32 devices in a mesh: sect: 4 (over y, x), dom: 8 (over z, core).
Axes of the slice: x: 2, y: 2, z: 4, core: 2. Of those that a mesh axis runs over, the one named last changes fastest.
Arguments:
- cells: int32 [3, 4, 8, 256], P(None, 'sect', 'dom'), may hold values from 0 to 255, as said below
- fracs: float32 [3, 4, 8, 256], P(None, 'sect', 'dom'), may hold values from 0 to 1
- charges: float32 [4, 8, 256], P('sect', 'dom'), may hold values from -1 to 1
- pair_blocks: int32 [4, 8, 2, 8], P('sect', 'dom'), may hold values from 0 to 17
- influence: float32 [256, 256, 256], P('dom', 'sect'), may hold values from 1 to 100
Outputs:
- forces: float32 [3, 4, 8, 256], P(None, 'sect', 'dom')
The draws below stay inside these ranges and needn't reach their ends.
Inputs may be any that keep to these rules, and one draw needn't show every extreme that they name: On device (s, d), cells[0] lies in [s * 64, (s + 1) * 64) and cells[2] in [d * 32, (d + 1) * 32). With owner = cells[1] // 32, each device's atoms come in order of ascending owner, no owner has more than 64 atoms of one device, and for each index of sect one owner has exactly 64 atoms of every device of that index.
All inputs are finite; a program needn't handle non-finite values.
Results may differ from the reference program's by a relative error of at most 0.0003.
Values sent between devices are 32-bit elements; how exact they have to be, the bound alone decides.
No kernel may reach another device: no remote copies, remote signals or barrier semaphores. Data moves between devices by JAX's collectives and lax.ppermute only.
A program may use at most 128 MiB of HBM per device.

```python
import math
import jax
import jax.numpy as jnp
from jax import lax

MESH = 256
ATOM_DEV = 256
BLOCK = 128
NJ = 8
NB = 2
CAP = 64
XW = 64
YW = 32
N_SECT = 4
N_DOM = 8


def draw_cells(key, part):
    key_hot, key_bump, key_first, key_second, key_third = jax.random.split(key, 5)
    hottest = jax.random.randint(key_hot, (N_SECT, 1, 1), 0, N_DOM)
    remaining = ATOM_DEV - CAP
    ordinal = jnp.arange(remaining, dtype=jnp.int32)
    bumps = jax.random.randint(key_bump, (N_SECT, N_DOM, remaining), 0, 2)
    others = (hottest + 1 + jnp.mod(ordinal + bumps, N_DOM - 1)) % N_DOM
    owners = jnp.concatenate([jnp.broadcast_to(hottest, (N_SECT, N_DOM, CAP)), others], axis=2)
    owners = jnp.sort(owners, axis=2)
    shape = (N_SECT, N_DOM, ATOM_DEV)
    sect_rows = jnp.arange(N_SECT, dtype=jnp.int32).reshape(N_SECT, 1, 1)
    dom_rows = jnp.arange(N_DOM, dtype=jnp.int32).reshape(1, N_DOM, 1)
    first = sect_rows * XW + jax.random.randint(key_first, shape, 0, XW)
    second = owners * YW + jax.random.randint(key_second, shape, 0, YW)
    third = dom_rows * YW + jax.random.randint(key_third, shape, 0, YW)
    return jnp.stack([first, second, third]).astype(jnp.int32)


def plant(entries, rng, least, largest):
    dims = entries.shape
    index_at = [jax.random.randint(jax.random.fold_in(rng, axis), (), 0, dims[axis]) for axis in range(len(dims))]
    entries = entries.at[tuple(index_at)].set(least)
    longest = dims.index(max(dims))
    index_at[longest] = (index_at[longest] + 1) % dims[longest]
    return entries.at[tuple(index_at)].set(largest)


def level_of(rng, extent, cuts, least, high):
    gain = 1.0
    for dim, parts in cuts:
        steps = jax.random.uniform(jax.random.fold_in(jax.random.fold_in(rng, 6), dim), (parts,), jnp.float32, least / len(cuts), high / len(cuts))
        gain = gain * jnp.repeat(jnp.exp(steps), extent[dim] // parts).reshape((-1,) + (1,) * (len(extent) - 1 - dim))
    return gain


def setup_inputs(seed: int = 0) -> dict:
    arg_keys = jax.random.split(jax.random.key(seed), 6)
    cells = draw_cells(jax.random.fold_in(arg_keys[5], 71), 0)
    fracs = jnp.clip(1.0 * jax.random.uniform(arg_keys[1], (3, N_SECT, N_DOM, ATOM_DEV), jnp.float32) ** level_of(arg_keys[1], (3, N_SECT, N_DOM, ATOM_DEV), ((1, 4), (2, 8)), -0.2, 0.2), 0.0, 1.0)
    charges = jnp.clip(jax.random.uniform(arg_keys[2], (N_SECT, N_DOM, ATOM_DEV), jnp.float32, -1.0, 1.0) * level_of(arg_keys[2], (N_SECT, N_DOM, ATOM_DEV), ((0, 4), (1, 8)), -0.4, 0.0), -1.0, 1.0)
    pair_blocks = plant(jax.random.randint(arg_keys[3], (N_SECT, N_DOM, NB, NJ), 0, 9 * NB), jax.random.fold_in(arg_keys[3], 1), 0, (9 * NB) - 1).astype(jnp.int32)
    influence = jnp.clip(jnp.exp(math.log(100.0) - 4.6051702 * jax.random.uniform(arg_keys[4], (MESH, MESH, MESH), jnp.float32) ** level_of(arg_keys[4], (MESH, MESH, MESH), ((0, 8), (1, 4)), -0.2, 0.2)), 1.0, 100.0)
    return {"cells": cells, "fracs": fracs, "charges": charges, "pair_blocks": pair_blocks, "influence": influence}


ewald_beta = 0.1
soft_square = 9.0

def spline_weights(frac):
    inner = 1.0 - frac
    square = frac * frac
    cube = square * frac
    weights = jnp.stack([inner * inner * inner / 6.0, (3.0 * cube - 6.0 * square + 4.0) / 6.0, (-3.0 * cube + 3.0 * square + 3.0 * frac + 1.0) / 6.0, cube / 6.0])
    slopes = jnp.stack([-inner * inner / 2.0, (3.0 * square - 4.0 * frac) / 2.0, (-3.0 * square + 2.0 * frac + 1.0) / 2.0, square / 2.0])
    return (weights, slopes)

def pair_kernel(centre, others, mesh_size):
    half_mesh = float(mesh_size // 2)
    displace = []
    for component in range(3):
        offset = centre[component][None, :, None] - others[component][:, None, :]
        wrapped = jnp.mod(offset + half_mesh, float(mesh_size)) - half_mesh
        displace.append(wrapped + (centre[component + 3][None, :, None] - others[component + 3][:, None, :]))
    square = displace[0] * displace[0] + displace[1] * displace[1] + displace[2] * displace[2] + soft_square
    distance = jnp.sqrt(square)
    kernel = lax.erfc(ewald_beta * distance) / (square * distance) + 2.0 * ewald_beta / math.sqrt(math.pi) * jnp.exp(-ewald_beta * ewald_beta * square) / square
    coupling = centre[6][None, :, None] * others[6][:, None, :] * kernel
    return jnp.stack([lax.optimization_barrier(jnp.sum(coupling * shift_vector, axis=(0, 2))) for shift_vector in displace])

def reference(cells, fracs, charges, pair_blocks, influence):
    atoms = jnp.concatenate([cells.astype(jnp.float32), fracs, charges[None]], axis=0)
    neighbours = []
    for shift_sect in (-1, 0, 1):
        for shift_dom in (-1, 0, 1):
            neighbours.append(jnp.roll(atoms, (-shift_sect, -shift_dom), axis=(1, 2)))
    beside_all = jnp.stack(neighbours, axis=1)
    beside_all = jnp.transpose(beside_all, (2, 3, 0, 1, 4)).reshape(N_SECT * N_DOM, 7, 9 * NB, BLOCK)
    own_blocks = jnp.transpose(atoms, (1, 2, 0, 3)).reshape(N_SECT * N_DOM, 7, NB, BLOCK)
    lists = pair_blocks.reshape(N_SECT * N_DOM, NB * NJ)

    def per_device(items):
        own_dev, around_dev, list_dev = items
        listed = around_dev[:, list_dev].reshape(7, NB, NJ, BLOCK)

        def per_block(pieces):
            return pair_kernel(pieces[0], pieces[1], MESH)
        block_forces = lax.map(per_block, (jnp.moveaxis(own_dev, 1, 0), jnp.moveaxis(listed, 1, 0)))
        return jnp.transpose(block_forces, (1, 0, 2)).reshape(3, ATOM_DEV)
    short_force = lax.map(per_device, (own_blocks, beside_all, lists))
    short_force = jnp.transpose(short_force.reshape(N_SECT, N_DOM, 3, ATOM_DEV), (2, 0, 1, 3))
    offsets = jnp.arange(4, dtype=jnp.int32)
    spans = [(cells[axis_pos].reshape(-1)[None, :] + offsets[:, None]) % MESH for axis_pos in range(3)]
    stencil = (spans[0][:, None, None, :] * MESH + spans[1][None, :, None, :]) * MESH + spans[2][None, None, :, :]
    splines = [spline_weights(fracs[axis_pos].reshape(-1)) for axis_pos in range(3)]
    charge = charges.reshape(-1)
    values = charge[None, None, None, :] * splines[0][0][:, None, None, :] * splines[1][0][None, :, None, :] * splines[2][0][None, None, :, :]
    grid = jnp.zeros((MESH * MESH * MESH,), jnp.float32).at[stencil.reshape(-1)].add(values.reshape(-1))
    spectrum = jnp.fft.fftn(grid.reshape(MESH, MESH, MESH))
    kernel_xyz = jnp.transpose(influence, (2, 1, 0))
    potential = jnp.real(jnp.fft.ifftn(spectrum * kernel_xyz)).astype(jnp.float32)
    samples = potential.reshape(-1)[stencil]
    weights = [entry[0] for entry in splines]
    slopes = [entry[1] for entry in splines]
    first = lax.optimization_barrier(jnp.sum(slopes[0][:, None, None, :] * weights[1][None, :, None, :] * weights[2][None, None, :, :] * samples, axis=(0, 1, 2)))
    second = lax.optimization_barrier(jnp.sum(weights[0][:, None, None, :] * slopes[1][None, :, None, :] * weights[2][None, None, :, :] * samples, axis=(0, 1, 2)))
    third = lax.optimization_barrier(jnp.sum(weights[0][:, None, None, :] * weights[1][None, :, None, :] * slopes[2][None, None, :, :] * samples, axis=(0, 1, 2)))
    mesh_force = (-charge * jnp.stack([first, second, third])).reshape(3, N_SECT, N_DOM, ATOM_DEV)
    return short_force + mesh_force
```

```python
import math

import jax
import jax.numpy as jnp
import numpy as np
from jax import lax
from jax.experimental import pallas as pl
from jax.experimental.pallas import tpu as pltpu
from jax.sharding import PartitionSpec as P

BLOCK = 128
XROWS = 8
CHUNKS = 2
VMEM = 56 * 1024 * 1024

ewald_beta = 0.1
soft_square = 9.0


def split_table(table):
    table = jnp.asarray(np.asarray(table, np.float32))
    high = table.astype(jnp.bfloat16)
    low = (table - high.astype(jnp.float32)).astype(jnp.bfloat16)
    return high, low


def split(value):
    high = value.astype(jnp.bfloat16)
    low = (value - high.astype(jnp.float32)).astype(jnp.bfloat16)
    return high, low


def dot(left, right, right_dim=0):
    return lax.dot_general(
        left, right, (((1,), (right_dim,)), ((), ())), preferred_element_type=jnp.float32
    )


def dot3(left, right, right_dim=0):
    return (
        dot(left[0], right[0], right_dim)
        + dot(left[0], right[1], right_dim)
        + dot(left[1], right[0], right_dim)
    )


def spline(frac):
    inner = 1.0 - frac
    square = frac * frac
    cube = square * frac
    weights = (
        inner * inner * inner / 6.0,
        (3.0 * cube - 6.0 * square + 4.0) / 6.0,
        (-3.0 * cube + 3.0 * square + 3.0 * frac + 1.0) / 6.0,
        cube / 6.0,
    )
    slopes = (
        -inner * inner / 2.0,
        (3.0 * square - 4.0 * frac) / 2.0,
        (-3.0 * square + 2.0 * frac + 1.0) / 2.0,
        square / 2.0,
    )
    return weights, slopes


def turn(steps, mesh_size):
    part = steps * (1.0 / mesh_size)
    part = part - jnp.floor(part)
    half = math.pi * jnp.where(part > 0.5, part - 1.0, part)
    sq = half * half
    sin = half
    cos = jnp.ones_like(half)
    term = half
    for n in range(1, 7):
        term = term * sq * (-1.0 / ((2 * n) * (2 * n + 1)))
        sin = sin + term
    term = cos
    for n in range(1, 8):
        term = term * sq * (-1.0 / ((2 * n - 1) * (2 * n)))
        cos = cos + term
    return 1.0 - 2.0 * sin * sin, 2.0 * sin * cos


def place(offset, values):
    out = jnp.zeros_like(offset)
    for k in range(4):
        out = jnp.where(offset == float(k), values[k], out)
    return out


def basis_kernel(mesh_size, z_width, slots_padded, where_ref, atoms, wx, vx, zq, zv, bwh, bwl, bvh, bvl):
    def row(n):
        return atoms[n : n + 1, :]

    lanes = atoms.shape[1]
    charge = row(6)

    def rows(count):
        return lax.broadcasted_iota(jnp.int32, (count, lanes), 0).astype(jnp.float32)

    weights, slopes = spline(row(3))
    offset = rows(wx.shape[0]) - row(0)
    wx[...] = place(offset, weights)
    vx[...] = place(offset, slopes)
    weights, slopes = spline(row(4))
    offset = rows(mesh_size) - row(1)
    offset = jnp.where(offset < 0.0, offset + mesh_size, offset)
    high, low = split(place(offset, weights))
    bwh[...] = high
    bwl[...] = low
    high, low = split(place(offset, slopes))
    bvh[...] = high
    bvl[...] = low
    weights, slopes = spline(row(5))
    wave = rows(slots_padded) + (where_ref[1] * z_width).astype(jnp.float32)
    parts = [jnp.zeros_like(wave) for _ in range(4)]
    for k in range(4):
        cos, sin = turn(wave * (row(2) + float(k)), mesh_size)
        parts[0] = parts[0] + (charge * weights[k]) * cos
        parts[1] = parts[1] - (charge * weights[k]) * sin
        parts[2] = parts[2] + (charge * slopes[k]) * cos
        parts[3] = parts[3] - (charge * slopes[k]) * sin
    zq[0:slots_padded, :] = parts[0]
    zq[slots_padded:, :] = parts[1]
    zv[0:slots_padded, :] = parts[2]
    zv[slots_padded:, :] = parts[3]


def spread_kernel(first, count, slots_padded, wx, zq, bwh, bwl, rh, rl, ih, il, out, acc):
    step = pl.program_id(0)
    rows = count * wx.shape[0]
    wide = wx[...]
    pieces = []
    for c in range(2):
        for g in range(count):
            at = c * slots_padded + first + g
            pieces.append(wide * zq[at : at + 1, :])
    left = split(jnp.concatenate(pieces, axis=0))
    part = dot3(left, (bwh[...], bwl[...]), 1)

    @pl.when(step == 0)
    def _():
        acc[...] = part

    @pl.when(step != 0)
    def _():
        acc[...] += part

    @pl.when(step == pl.num_programs(0) - 1)
    def _():
        real = split(acc[0:rows, :])
        imag = split(acc[rows:, :])
        lines = dot3(real, (rh[...], rl[...])) + dot3(imag, (ih[...], il[...]))
        lanes = out.shape[3]
        for s in range(out.shape[0]):
            out[s] = lines[:, s * lanes : (s + 1) * lanes].reshape(out.shape[1:])


def influence_kernel(scale, where_ref, own, across, edge, flip, same, back, out):
    slot = pl.program_id(0)
    own_pair = split(jnp.concatenate([own[0], own[0]], axis=0))
    across_pair = split(across[0])
    turned = dot(flip[...], across_pair[0]) + dot(flip[...], across_pair[1])
    lines = lax.broadcasted_iota(jnp.int32, turned.shape, 0) % own.shape[1]
    turned = split(jnp.where(lines == 0, edge[0], turned))
    plain = dot(same[...], own_pair[0], 1) + dot(same[...], own_pair[1], 1)
    mirror = dot(back[...], turned[0], 1) + dot(back[...], turned[1], 1)
    last = slot == pl.num_programs(0) - 1
    upper = where_ref[2] == 1
    keep_own = jnp.where(jnp.logical_and(last, jnp.logical_not(upper)), 0.0, scale)
    keep_mirror = jnp.where(slot == 0, 0.0, keep_own)
    out[0] = plain * keep_own + mirror * keep_mirror


def filter_kernel(lines, factor, th, tl, out):
    sects, count, extent, lanes = lines.shape
    width = extent - XROWS
    mesh_size = sects * width
    table = (th[...], tl[...])
    columns = []
    for g in range(count):
        pieces = []
        for s in range(sects):
            body = lines[s, g]
            before = lines[(s - 1) % sects, g, width:extent, :]
            pieces.append(body[0:XROWS] + before)
            pieces.append(body[XROWS:width])
        columns.append(jnp.concatenate(pieces, axis=0))
    both = dot3(table, split(jnp.concatenate(columns, axis=1)))
    half = lanes // 2
    sign = jnp.where(
        lax.broadcasted_iota(jnp.int32, (mesh_size, lanes), 1) < half, 1.0, -1.0
    )
    columns = []
    for g in range(count):
        cos = both[0:mesh_size, g * lanes : (g + 1) * lanes]
        sin = both[mesh_size:, g * lanes : (g + 1) * lanes]
        columns.append((cos + sign * pltpu.roll(sin, half, 1)) * factor[g])
    both = dot3(table, split(jnp.concatenate(columns, axis=1)))
    for g in range(count):
        cos = both[0:mesh_size, g * lanes : (g + 1) * lanes]
        sin = both[mesh_size:, g * lanes : (g + 1) * lanes]
        field = cos - sign * pltpu.roll(sin, half, 1)
        for s in range(sects):
            after = ((s + 1) % sects) * width
            out[s, g, 0:width, :] = field[s * width : (s + 1) * width]
            out[s, g, width:extent, :] = field[after : after + XROWS]


def gather_kernel(first, count, slots_padded, lines, bh, bl, wx, vx, zq, zv, bwh, bwl, bvh, bvl, out, eh, el):
    sects, _, extent, lanes = lines.shape
    rows = count * extent
    mesh_size = bwh.shape[0]

    @pl.when(pl.program_id(0) == 0)
    def _():
        joined = jnp.concatenate([lines[s].reshape(rows, lanes) for s in range(sects)], axis=1)
        field = dot3(split(joined), (bh[...], bl[...]))
        field = jnp.concatenate([field[:, 0:mesh_size], field[:, mesh_size:]], axis=0)
        high, low = split(field)
        eh[...] = high
        el[...] = low

    left = (eh[...], el[...])
    along = dot3(left, (bwh[...], bwl[...]))
    slope = dot3(left, (bvh[...], bvl[...]))
    sums = [jnp.zeros(wx.shape, jnp.float32) for _ in range(3)]
    for c in range(2):
        for g in range(count):
            at = c * slots_padded + first + g
            low = (c * count + g) * extent
            line = along[low : low + extent]
            sums[0] = sums[0] + line * zq[at : at + 1, :]
            sums[1] = sums[1] + slope[low : low + extent] * zq[at : at + 1, :]
            sums[2] = sums[2] + line * zv[at : at + 1, :]
    out[0:1, :] = -jnp.sum(sums[0] * vx[...], axis=0, keepdims=True)
    out[1:2, :] = -jnp.sum(sums[1] * wx[...], axis=0, keepdims=True)
    out[2:3, :] = -jnp.sum(sums[2] * wx[...], axis=0, keepdims=True)
    out[3:, :] = jnp.zeros((out.shape[0] - 3, out.shape[1]), jnp.float32)


def params():
    return pltpu.CompilerParams(vmem_limit_bytes=VMEM)


def whole(array):
    return pl.BlockSpec(array.shape, lambda *_: (0,) * array.ndim)


def along_atoms(rows, step):
    return pl.BlockSpec((rows, step), lambda n: (0, n))


SMEM = pl.BlockSpec(memory_space=pltpu.SMEM)


def pair_kernel(centre, others, mesh_size):
    half_mesh = float(mesh_size // 2)
    displace = []
    for component in range(3):
        offset = centre[component][None, :, None] - others[component][:, None, :]
        wrapped = jnp.mod(offset + half_mesh, float(mesh_size)) - half_mesh
        displace.append(
            wrapped + (centre[component + 3][None, :, None] - others[component + 3][:, None, :])
        )
    square = (
        displace[0] * displace[0]
        + displace[1] * displace[1]
        + displace[2] * displace[2]
        + soft_square
    )
    distance = jnp.sqrt(square)
    kernel = (
        lax.erfc(ewald_beta * distance) / (square * distance)
        + 2.0
        * ewald_beta
        / math.sqrt(math.pi)
        * jnp.exp(-ewald_beta * ewald_beta * square)
        / square
    )
    coupling = centre[6][None, :, None] * others[6][:, None, :] * kernel
    return jnp.stack([jnp.sum(coupling * shift_vector, axis=(0, 2)) for shift_vector in displace])


def shards(cells, fracs, charges, pair_blocks, influence):
    sects = lax.axis_size("sect")
    doms = lax.axis_size("dom")
    sect = lax.axis_index("sect")
    dom = lax.axis_index("dom")
    z_width, x_width, mesh_size = influence.shape
    atom_count = charges.shape[2]
    block_count = atom_count // BLOCK
    listed_count = pair_blocks.shape[3]
    half = z_width // 2
    slots = half + 1
    slots_padded = -(-slots // 8) * 8
    extent = x_width + XROWS
    lanes = 2 * x_width
    total = doms * atom_count
    where_am_i = jnp.stack([sect, dom, (dom >= doms // 2).astype(jnp.int32)])

    packed = jnp.concatenate(
        [cells.astype(jnp.float32), fracs, charges[None], jnp.zeros_like(charges)[None]], axis=0
    ).reshape(8, block_count, BLOCK)
    packed = jnp.transpose(packed, (1, 0, 2))
    everyone = lax.all_gather(packed, ("sect", "dom"))
    row = lax.dynamic_index_in_dim(
        everyone.reshape(sects, doms, block_count, 8, BLOCK), sect, 0, keepdims=False
    )
    atoms = jnp.transpose(row, (2, 0, 1, 3)).reshape(8, total)
    first_cell = jnp.zeros((8, 1), jnp.float32).at[0, 0].set(1.0) * (sect * x_width).astype(jnp.float32)
    atoms = atoms - first_cell

    opposite = []
    edges = []
    for s in range(sects):
        for d in range(doms):
            opposite.append((s * doms + d, (sects - 1 - s) * doms + doms - 1 - d))
            edges.append((s * doms + d, ((sects - s) % sects) * doms + doms - 1 - d))
    across = lax.ppermute(influence[half:], ("sect", "dom"), opposite)
    edge = lax.ppermute(influence[half:, 0:1], ("sect", "dom"), edges)
    flip = np.zeros((2 * x_width, x_width), np.float32)
    for i in range(1, x_width):
        flip[i, x_width - i] = 1.0
        flip[x_width + i, x_width - i] = 1.0
    same = np.eye(mesh_size, dtype=np.float32)
    back = np.roll(same[::-1], 1, axis=0)
    flip, same, back = (jnp.asarray(m).astype(jnp.bfloat16) for m in (flip, same, back))
    factor = pl.pallas_call(
        lambda *refs: influence_kernel(float(mesh_size) ** -3, *refs),
        grid=(slots,),
        in_specs=[
            SMEM,
            pl.BlockSpec((1, x_width, mesh_size), lambda j: (j, 0, 0)),
            pl.BlockSpec((1, x_width, mesh_size), lambda j: (jnp.minimum(half - j, half - 1), 0, 0)),
            pl.BlockSpec((1, 1, mesh_size), lambda j: (jnp.minimum(half - j, half - 1), 0, 0)),
            whole(flip),
            whole(same),
            whole(back),
        ],
        out_specs=pl.BlockSpec((1, mesh_size, lanes), lambda j: (j, 0, 0)),
        out_shape=jax.ShapeDtypeStruct((slots, mesh_size, lanes), jnp.float32),
        compiler_params=params(),
        name="influence",
    )(where_am_i, influence, across, edge, flip, same, back)

    step = np.arange(mesh_size)
    angle = 2.0 * np.pi * (np.outer(step, step) % mesh_size) / mesh_size
    cos, sin = np.cos(angle), np.sin(angle)

    def by_sect(real, imag):
        real = real.reshape(mesh_size, sects, 1, x_width)
        imag = imag.reshape(mesh_size, sects, 1, x_width)
        return np.concatenate([real, imag], axis=2).reshape(mesh_size, 2 * mesh_size)

    rh, rl = split_table(by_sect(cos, -sin))
    ih, il = split_table(by_sect(sin, cos))
    bh, bl = split_table(np.concatenate([by_sect(cos, -sin).T, by_sect(sin, cos).T], axis=1))
    th, tl = split_table(np.concatenate([cos, sin], axis=0))

    atom_step = 512
    grid = (total // atom_step,)
    f32, bf16 = jnp.float32, jnp.bfloat16
    shapes = [
        ((extent, total), f32),
        ((extent, total), f32),
        ((2 * slots_padded, total), f32),
        ((2 * slots_padded, total), f32),
    ] + [((mesh_size, total), bf16)] * 4
    wx, vx, zq, zv, bwh, bwl, bvh, bvl = pl.pallas_call(
        lambda *refs: basis_kernel(mesh_size, z_width, slots_padded, *refs),
        grid=grid,
        in_specs=[SMEM, along_atoms(8, atom_step)],
        out_specs=[along_atoms(shape[0], atom_step) for shape, _ in shapes],
        out_shape=[jax.ShapeDtypeStruct(shape, dtype) for shape, dtype in shapes],
        compiler_params=params(),
        name="basis",
    )(where_am_i, atoms)

    firsts = [slots * n // CHUNKS for n in range(CHUNKS + 1)]
    counts = [b - a for a, b in zip(firsts, firsts[1:])]
    sent = []
    for first, count in zip(firsts, counts):
        shape = (sects, count, extent, lanes)
        lines = pl.pallas_call(
            lambda *refs, first=first, count=count: spread_kernel(first, count, slots_padded, *refs),
            grid=grid,
            in_specs=[
                along_atoms(extent, atom_step),
                along_atoms(2 * slots_padded, atom_step),
                along_atoms(mesh_size, atom_step),
                along_atoms(mesh_size, atom_step),
            ]
            + [whole(t) for t in (rh, rl, ih, il)],
            out_specs=pl.BlockSpec(shape, lambda n: (0, 0, 0, 0)),
            out_shape=jax.ShapeDtypeStruct(shape, f32),
            scratch_shapes=[pltpu.VMEM((2 * count * extent, mesh_size), f32)],
            compiler_params=params(),
            name="spread",
        )(wx, zq, bwh, bwl, rh, rl, ih, il)
        sent.append(lax.all_to_all(lines, "sect", split_axis=0, concat_axis=0, tiled=True))
    fields = []
    for lines, first, count in zip(sent, firsts, counts):
        field = pl.pallas_call(
            filter_kernel,
            grid=(1,),
            in_specs=[
                whole(lines),
                pl.BlockSpec((count, mesh_size, lanes), lambda n: (0, 0, 0)),
                whole(th),
                whole(tl),
            ],
            out_specs=whole(lines),
            out_shape=jax.ShapeDtypeStruct(lines.shape, f32),
            compiler_params=params(),
            name="filter",
        )(lines, factor[first : first + count], th, tl)
        fields.append(lax.all_to_all(field, "sect", split_axis=0, concat_axis=0, tiled=True))

    listed = pair_blocks[0, 0]
    neighbour = listed // block_count
    from_sect = (sect + neighbour // 3 - 1) % sects
    from_dom = (dom + neighbour % 3 - 1) % doms
    source = (from_sect * doms + from_dom) * block_count + listed % block_count
    pool = everyone.reshape(sects * doms * block_count, 8 * BLOCK)
    pick = (source.reshape(-1, 1) == jnp.arange(pool.shape[0], dtype=jnp.int32)[None]).astype(f32)
    chosen = lax.dot_general(
        pick, pool, (((1,), (0,)), ((), ())), precision=lax.Precision.HIGHEST, preferred_element_type=f32
    ).reshape(block_count, listed_count, 8, BLOCK)
    chosen = jnp.transpose(chosen, (0, 2, 1, 3))
    block_forces = jnp.stack(
        [pair_kernel(packed[b], chosen[b], mesh_size) for b in range(block_count)], axis=1
    )
    short_force = block_forces.reshape(3, atom_count)

    partial = None
    for lines, first, count in zip(fields, firsts, counts):
        forces = pl.pallas_call(
            lambda *refs, first=first, count=count: gather_kernel(first, count, slots_padded, *refs),
            grid=grid,
            in_specs=[whole(lines), whole(bh), whole(bl)]
            + [along_atoms(a.shape[0], atom_step) for a in (wx, vx, zq, zv, bwh, bwl, bvh, bvl)],
            out_specs=along_atoms(8, atom_step),
            out_shape=jax.ShapeDtypeStruct((8, total), f32),
            scratch_shapes=[pltpu.VMEM((2 * count * extent, mesh_size), bf16)] * 2,
            compiler_params=params(),
            name="gather",
        )(lines, bh, bl, wx, vx, zq, zv, bwh, bwl, bvh, bvl)
        partial = forces if partial is None else partial + forces
    by_dom = jnp.transpose(partial[:3].reshape(3, doms, atom_count), (1, 0, 2))
    mesh_force = lax.psum_scatter(by_dom, "dom", scatter_dimension=0, tiled=False)
    return (short_force + mesh_force).reshape(3, 1, 1, atom_count)


def solution(mesh):
    in_specs = (
        P(None, "sect", "dom", None),
        P(None, "sect", "dom", None),
        P("sect", "dom", None),
        P("sect", "dom", None, None),
        P("dom", "sect", None),
    )
    out_specs = P(None, "sect", "dom", None)
    return jax.shard_map(shards, mesh=mesh, in_specs=in_specs, out_specs=out_specs, check_vma=False)
```

```python
import math

import jax
import jax.numpy as jnp
import numpy as np
from jax import lax
from jax.experimental import pallas as pl
from jax.experimental.pallas import tpu as pltpu
from jax.sharding import PartitionSpec as P

BLOCK = 128
XROWS = 8
CHUNKS = 2
VMEM = 56 * 1024 * 1024

ewald_beta = 0.1
soft_square = 9.0


def split_table(table):
    table = jnp.asarray(np.asarray(table, np.float32))
    high = table.astype(jnp.bfloat16)
    low = (table - high.astype(jnp.float32)).astype(jnp.bfloat16)
    return high, low


def split(value):
    high = value.astype(jnp.bfloat16)
    low = (value - high.astype(jnp.float32)).astype(jnp.bfloat16)
    return high, low


def dot(left, right, right_dim=0):
    return lax.dot_general(
        left, right, (((1,), (right_dim,)), ((), ())), preferred_element_type=jnp.float32
    )


def dot3(left, right, right_dim=0):
    return (
        dot(left[0], right[0], right_dim)
        + dot(left[0], right[1], right_dim)
        + dot(left[1], right[0], right_dim)
    )


def spline(frac):
    inner = 1.0 - frac
    square = frac * frac
    cube = square * frac
    weights = (
        inner * inner * inner / 6.0,
        (3.0 * cube - 6.0 * square + 4.0) / 6.0,
        (-3.0 * cube + 3.0 * square + 3.0 * frac + 1.0) / 6.0,
        cube / 6.0,
    )
    slopes = (
        -inner * inner / 2.0,
        (3.0 * square - 4.0 * frac) / 2.0,
        (-3.0 * square + 2.0 * frac + 1.0) / 2.0,
        square / 2.0,
    )
    return weights, slopes


def turn(steps, mesh_size):
    part = steps * (1.0 / mesh_size)
    part = part - jnp.floor(part)
    half = math.pi * jnp.where(part > 0.5, part - 1.0, part)
    sq = half * half
    sin = half
    cos = jnp.ones_like(half)
    term = half
    for n in range(1, 7):
        term = term * sq * (-1.0 / ((2 * n) * (2 * n + 1)))
        sin = sin + term
    term = cos
    for n in range(1, 8):
        term = term * sq * (-1.0 / ((2 * n - 1) * (2 * n)))
        cos = cos + term
    return 1.0 - 2.0 * sin * sin, 2.0 * sin * cos


def place(offset, values):
    out = jnp.zeros_like(offset)
    for k in range(4):
        out = jnp.where(offset == float(k), values[k], out)
    return out


def basis_kernel(mesh_size, x_width, z_width, slots_padded, where_ref, blocks, wx, vx, zq, zv, bwh, bwl, bvh, bvl):
    atoms = jnp.concatenate(
        [blocks[d, b] for d in range(blocks.shape[0]) for b in range(blocks.shape[1])], axis=1
    )

    def row(n):
        return atoms[n : n + 1, :]

    lanes = atoms.shape[1]
    charge = row(6)

    def rows(count):
        return lax.broadcasted_iota(jnp.int32, (count, lanes), 0).astype(jnp.float32)

    weights, slopes = spline(row(3))
    offset = rows(wx.shape[0]) - (row(0) - (where_ref[0] * x_width).astype(jnp.float32))
    wx[...] = place(offset, weights)
    vx[...] = place(offset, slopes)
    weights, slopes = spline(row(4))
    offset = rows(mesh_size) - row(1)
    offset = jnp.where(offset < 0.0, offset + mesh_size, offset)
    high, low = split(place(offset, weights))
    bwh[...] = high
    bwl[...] = low
    high, low = split(place(offset, slopes))
    bvh[...] = high
    bvl[...] = low
    weights, slopes = spline(row(5))
    wave = rows(slots_padded) + (where_ref[1] * z_width).astype(jnp.float32)
    parts = [jnp.zeros_like(wave) for _ in range(4)]
    for k in range(4):
        cos, sin = turn(wave * (row(2) + float(k)), mesh_size)
        parts[0] = parts[0] + (charge * weights[k]) * cos
        parts[1] = parts[1] - (charge * weights[k]) * sin
        parts[2] = parts[2] + (charge * slopes[k]) * cos
        parts[3] = parts[3] - (charge * slopes[k]) * sin
    zq[0:slots_padded, :] = parts[0]
    zq[slots_padded:, :] = parts[1]
    zv[0:slots_padded, :] = parts[2]
    zv[slots_padded:, :] = parts[3]


def spread_kernel(first, count, slots_padded, wx, zq, bwh, bwl, rh, rl, ih, il, out, acc):
    step = pl.program_id(0)
    rows = count * wx.shape[0]
    wide = wx[...]
    pieces = []
    for c in range(2):
        for g in range(count):
            at = c * slots_padded + first + g
            pieces.append(wide * zq[at : at + 1, :])
    left = split(jnp.concatenate(pieces, axis=0))
    part = dot3(left, (bwh[...], bwl[...]), 1)

    @pl.when(step == 0)
    def _():
        acc[...] = part

    @pl.when(step != 0)
    def _():
        acc[...] += part

    @pl.when(step == pl.num_programs(0) - 1)
    def _():
        real = split(acc[0:rows, :])
        imag = split(acc[rows:, :])
        lines = dot3(real, (rh[...], rl[...])) + dot3(imag, (ih[...], il[...]))
        lanes = out.shape[3]
        for s in range(out.shape[0]):
            out[s] = lines[:, s * lanes : (s + 1) * lanes].reshape(out.shape[1:])


def influence_kernel(first, half, scale, where_ref, own, across, edge, flip, same, back, out):
    count, _, lanes = out.shape
    width = own.shape[1]
    lowest = half - max(first + count - 1, 1)
    plain = [own[first + g] for g in range(count) for _ in range(2)]
    plain = split(jnp.concatenate(plain, axis=0))
    pieces = []
    for g in range(count):
        at = half - max(first + g, 1)
        pair = split(across[at - lowest])
        turned = dot(flip[...], pair[0]) + dot(flip[...], pair[1])
        lines = lax.broadcasted_iota(jnp.int32, turned.shape, 0) % width
        pieces.append(jnp.where(lines == 0, edge[at], turned))
    turned = split(jnp.concatenate(pieces, axis=0))
    plain = dot(same[...], plain[0], 1) + dot(same[...], plain[1], 1)
    mirror = dot(back[...], turned[0], 1) + dot(back[...], turned[1], 1)
    for g in range(count):
        keep = scale
        if first + g == half:
            keep = jnp.where(where_ref[2] == 1, scale, 0.0)
        value = plain[:, g * lanes : (g + 1) * lanes]
        if first + g > 0:
            value = value + mirror[:, g * lanes : (g + 1) * lanes]
        out[g] = value * keep


def filter_kernel(lines, factor, th, tl, out):
    sects, count, extent, lanes = lines.shape
    width = extent - XROWS
    mesh_size = sects * width
    table = (th[...], tl[...])
    columns = []
    for g in range(count):
        pieces = []
        for s in range(sects):
            body = lines[s, g]
            before = lines[(s - 1) % sects, g, width:extent, :]
            pieces.append(body[0:XROWS] + before)
            pieces.append(body[XROWS:width])
        columns.append(jnp.concatenate(pieces, axis=0))
    both = dot3(table, split(jnp.concatenate(columns, axis=1)))
    half = lanes // 2
    sign = jnp.where(
        lax.broadcasted_iota(jnp.int32, (mesh_size, lanes), 1) < half, 1.0, -1.0
    )
    columns = []
    for g in range(count):
        cos = both[0:mesh_size, g * lanes : (g + 1) * lanes]
        sin = both[mesh_size:, g * lanes : (g + 1) * lanes]
        columns.append((cos + sign * pltpu.roll(sin, half, 1)) * factor[g])
    both = dot3(table, split(jnp.concatenate(columns, axis=1)))
    for g in range(count):
        cos = both[0:mesh_size, g * lanes : (g + 1) * lanes]
        sin = both[mesh_size:, g * lanes : (g + 1) * lanes]
        field = cos - sign * pltpu.roll(sin, half, 1)
        for s in range(sects):
            after = ((s + 1) % sects) * width
            out[s, g, 0:width, :] = field[s * width : (s + 1) * width]
            out[s, g, width:extent, :] = field[after : after + XROWS]


def gather_kernel(first, count, slots_padded, lines, bh, bl, wx, vx, zq, zv, bwh, bwl, bvh, bvl, *rest):
    *earlier, out, eh, el = rest
    sects, _, extent, lanes = lines.shape
    rows = count * extent
    mesh_size = bwh.shape[0]

    @pl.when(pl.program_id(0) == 0)
    def _():
        joined = jnp.concatenate([lines[s].reshape(rows, lanes) for s in range(sects)], axis=1)
        field = dot3(split(joined), (bh[...], bl[...]))
        field = jnp.concatenate([field[:, 0:mesh_size], field[:, mesh_size:]], axis=0)
        high, low = split(field)
        eh[...] = high
        el[...] = low

    left = (eh[...], el[...])
    along = dot3(left, (bwh[...], bwl[...]))
    slope = dot3(left, (bvh[...], bvl[...]))
    sums = [jnp.zeros(wx.shape, jnp.float32) for _ in range(3)]
    for c in range(2):
        for g in range(count):
            at = c * slots_padded + first + g
            low = (c * count + g) * extent
            line = along[low : low + extent]
            sums[0] = sums[0] + line * zq[at : at + 1, :]
            sums[1] = sums[1] + slope[low : low + extent] * zq[at : at + 1, :]
            sums[2] = sums[2] + line * zv[at : at + 1, :]
    forces = [
        -jnp.sum(total * shape[...], axis=0, keepdims=True)
        for total, shape in zip(sums, (vx, wx, wx))
    ]
    result = jnp.concatenate(forces + [jnp.zeros_like(forces[0])], axis=0)
    width = out.shape[2]
    for d in range(out.shape[0]):
        part = result[:, d * width : (d + 1) * width]
        out[d] = part + earlier[0][d] if earlier else part


def cost(micros):
    return pl.CostEstimate(flops=int(micros * 1.0e9), transcendentals=0, bytes_accessed=int(micros * 1.0e5))


def params():
    return pltpu.CompilerParams(vmem_limit_bytes=VMEM)


def whole(array):
    return pl.BlockSpec(array.shape, lambda *_: (0,) * array.ndim)


def along_atoms(rows, step):
    return pl.BlockSpec((rows, step), lambda n: (0, n))


SMEM = pl.BlockSpec(memory_space=pltpu.SMEM)


def pair_kernel(centre, others, mesh_size):
    half_mesh = float(mesh_size // 2)
    displace = []
    for component in range(3):
        offset = centre[component][None, :, None] - others[component][:, None, :]
        wrapped = jnp.mod(offset + half_mesh, float(mesh_size)) - half_mesh
        displace.append(
            wrapped + (centre[component + 3][None, :, None] - others[component + 3][:, None, :])
        )
    square = (
        displace[0] * displace[0]
        + displace[1] * displace[1]
        + displace[2] * displace[2]
        + soft_square
    )
    distance = jnp.sqrt(square)
    kernel = (
        lax.erfc(ewald_beta * distance) / (square * distance)
        + 2.0
        * ewald_beta
        / math.sqrt(math.pi)
        * jnp.exp(-ewald_beta * ewald_beta * square)
        / square
    )
    coupling = centre[6][None, :, None] * others[6][:, None, :] * kernel
    return jnp.stack([jnp.sum(coupling * shift_vector, axis=(0, 2)) for shift_vector in displace])


def shards(cells, fracs, charges, pair_blocks, influence):
    sects = lax.axis_size("sect")
    doms = lax.axis_size("dom")
    sect = lax.axis_index("sect")
    dom = lax.axis_index("dom")
    z_width, x_width, mesh_size = influence.shape
    atom_count = charges.shape[2]
    block_count = atom_count // BLOCK
    listed_count = pair_blocks.shape[3]
    half = z_width // 2
    slots = half + 1
    slots_padded = -(-slots // 8) * 8
    extent = x_width + XROWS
    lanes = 2 * x_width
    total = doms * atom_count
    where_am_i = jnp.stack([sect, dom, (dom >= doms // 2).astype(jnp.int32)])

    packed = jnp.concatenate(
        [cells.astype(jnp.float32), fracs, charges[None], jnp.zeros_like(charges)[None]], axis=0
    ).reshape(8, block_count, BLOCK)
    packed = jnp.transpose(packed, (1, 0, 2))
    row = lax.all_to_all(
        jnp.broadcast_to(packed[None], (doms,) + packed.shape), "dom", 0, 0, tiled=True
    )

    edges = []
    for s in range(sects):
        for d in range(doms):
            edges.append((s * doms + d, ((sects - s) % sects) * doms + doms - 1 - d))
    flip = np.zeros((2 * x_width, x_width), np.float32)
    for i in range(1, x_width):
        flip[i, x_width - i] = 1.0
        flip[x_width + i, x_width - i] = 1.0
    same = np.eye(mesh_size, dtype=np.float32)
    back = np.roll(same[::-1], 1, axis=0)
    flip, same, back = (jnp.asarray(m).astype(jnp.bfloat16) for m in (flip, same, back))
    firsts = [slots * n // CHUNKS for n in range(CHUNKS + 1)]
    counts = [b - a for a, b in zip(firsts, firsts[1:])]
    planes = []
    for first, count in zip(firsts, counts):
        lowest = half - max(first + count - 1, 1)
        highest = half - max(first, 1)
        planes.append(influence[half + lowest : half + highest + 1])
    sect_flip = [(s, sects - 1 - s) for s in range(sects)]
    dom_flip = [(d, doms - 1 - d) for d in range(doms)]
    planes = [
        lax.ppermute(p, *(("dom", dom_flip) if n % 2 else ("sect", sect_flip)))
        for n, p in enumerate(planes)
    ]

    step = np.arange(mesh_size)
    angle = 2.0 * np.pi * (np.outer(step, step) % mesh_size) / mesh_size
    cos, sin = np.cos(angle), np.sin(angle)

    def by_sect(real, imag):
        real = real.reshape(mesh_size, sects, 1, x_width)
        imag = imag.reshape(mesh_size, sects, 1, x_width)
        return np.concatenate([real, imag], axis=2).reshape(mesh_size, 2 * mesh_size)

    rh, rl = split_table(by_sect(cos, -sin))
    ih, il = split_table(by_sect(sin, cos))
    bh, bl = split_table(np.concatenate([by_sect(cos, -sin).T, by_sect(sin, cos).T], axis=1))
    th, tl = split_table(np.concatenate([cos, sin], axis=0))

    atom_step = 512
    grid = (total // atom_step,)
    f32, bf16 = jnp.float32, jnp.bfloat16
    shapes = [
        ((extent, total), f32),
        ((extent, total), f32),
        ((2 * slots_padded, total), f32),
        ((2 * slots_padded, total), f32),
    ] + [((mesh_size, total), bf16)] * 4
    wx, vx, zq, zv, bwh, bwl, bvh, bvl = pl.pallas_call(
        lambda *refs: basis_kernel(mesh_size, x_width, z_width, slots_padded, *refs),
        grid=grid,
        in_specs=[
            SMEM,
            pl.BlockSpec((atom_step // atom_count, block_count, 8, BLOCK), lambda n: (n, 0, 0, 0)),
        ],
        out_specs=[along_atoms(shape[0], atom_step) for shape, _ in shapes],
        out_shape=[jax.ShapeDtypeStruct(shape, dtype) for shape, dtype in shapes],
        compiler_params=params(),
        cost_estimate=cost(6),
        name="basis",
    )(where_am_i, row)

    sent = []
    for first, count in zip(firsts, counts):
        shape = (sects, count, extent, lanes)
        lines = pl.pallas_call(
            lambda *refs, first=first, count=count: spread_kernel(first, count, slots_padded, *refs),
            grid=grid,
            in_specs=[
                along_atoms(extent, atom_step),
                along_atoms(2 * slots_padded, atom_step),
                along_atoms(mesh_size, atom_step),
                along_atoms(mesh_size, atom_step),
            ]
            + [whole(t) for t in (rh, rl, ih, il)],
            out_specs=pl.BlockSpec(shape, lambda n: (0, 0, 0, 0)),
            out_shape=jax.ShapeDtypeStruct(shape, f32),
            scratch_shapes=[pltpu.VMEM((2 * count * extent, mesh_size), f32)],
            compiler_params=params(),
            cost_estimate=cost(9),
            name="spread",
        )(wx, zq, bwh, bwl, rh, rl, ih, il)
        sent.append(lines)
    corner, beside, planes, sent[0] = lax.optimization_barrier(
        (influence[half:, 0:1], row, planes, sent[0])
    )
    planes = [
        lax.ppermute(p, *(("sect", sect_flip) if n % 2 else ("dom", dom_flip)))
        for n, p in enumerate(planes)
    ]
    edge = lax.ppermute(corner, ("sect", "dom"), edges)
    ahead = [(s, (s + 1) % sects) for s in range(sects)]
    behind = [(b, a) for a, b in ahead]
    near = [lax.ppermute(beside, "sect", ahead), lax.ppermute(beside, "sect", behind)]
    sent = [lax.all_to_all(lines, "sect", split_axis=0, concat_axis=0, tiled=True) for lines in sent]
    planes[0], edge, sent[0] = lax.optimization_barrier((planes[0], edge, sent[0]))
    factors = [
        pl.pallas_call(
            lambda *refs, first=first: influence_kernel(first, half, float(mesh_size) ** -3, *refs),
            in_specs=[SMEM] + [pl.BlockSpec(memory_space=pltpu.VMEM)] * 6,
            out_specs=pl.BlockSpec(memory_space=pltpu.VMEM),
            out_shape=jax.ShapeDtypeStruct((count, mesh_size, lanes), f32),
            compiler_params=params(),
            cost_estimate=cost(3.5),
            name="influence",
        )(where_am_i, influence, mirror, edge, flip, same, back)
        for first, count, mirror in zip(firsts, counts, planes)
    ]
    fields = []
    for lines, factor in zip(sent, factors):
        field = pl.pallas_call(
            filter_kernel,
            grid=(1,),
            in_specs=[
                whole(lines),
                whole(factor),
                whole(th),
                whole(tl),
            ],
            out_specs=whole(lines),
            out_shape=jax.ShapeDtypeStruct(lines.shape, f32),
            compiler_params=params(),
            cost_estimate=cost(5.5),
            name="filter",
        )(lines, factor, th, tl)
        fields.append(field)
    near, row, packed, fields[0] = lax.optimization_barrier((near, row, packed, fields[0]))
    fields = [lax.all_to_all(field, "sect", split_axis=0, concat_axis=0, tiled=True) for field in fields]

    listed = pair_blocks[0, 0]
    neighbour = listed // block_count
    near = jnp.stack([near[0], row, near[1]])
    from_dom = (dom + neighbour % 3 - 1) % doms
    source = (neighbour // 3 * doms + from_dom) * block_count + listed % block_count
    pool = near.reshape(3 * doms * block_count, 8 * BLOCK)
    pick = (source.reshape(-1, 1) == jnp.arange(pool.shape[0], dtype=jnp.int32)[None]).astype(f32)
    chosen = lax.dot_general(
        pick, pool, (((1,), (0,)), ((), ())), precision=lax.Precision.HIGHEST, preferred_element_type=f32
    ).reshape(block_count, listed_count, 8, BLOCK)
    chosen = jnp.transpose(chosen, (0, 2, 1, 3))
    block_forces = jnp.stack(
        [pair_kernel(packed[b], chosen[b], mesh_size) for b in range(block_count)], axis=1
    )
    short_force = block_forces.reshape(3, atom_count)

    earlier = []
    by_dom = pl.BlockSpec((atom_step // atom_count, 4, atom_count), lambda n: (n, 0, 0))
    for lines, first, count in zip(fields, firsts, counts):
        earlier = [pl.pallas_call(
            lambda *refs, first=first, count=count: gather_kernel(first, count, slots_padded, *refs),
            grid=grid,
            in_specs=[whole(lines), whole(bh), whole(bl)]
            + [along_atoms(a.shape[0], atom_step) for a in (wx, vx, zq, zv, bwh, bwl, bvh, bvl)]
            + [by_dom] * len(earlier),
            out_specs=by_dom,
            out_shape=jax.ShapeDtypeStruct((doms, 4, atom_count), f32),
            scratch_shapes=[pltpu.VMEM((2 * count * extent, mesh_size), bf16)] * 2,
            compiler_params=params(),
            cost_estimate=cost(13),
            name="gather",
        )(lines, bh, bl, wx, vx, zq, zv, bwh, bwl, bvh, bvl, *earlier)]
    shares = lax.all_to_all(earlier[0], "dom", 0, 0, tiled=True)
    mesh_force = jnp.sum(shares, axis=0)[:3]
    return (short_force + mesh_force).reshape(3, 1, 1, atom_count)


def solution(mesh):
    in_specs = (
        P(None, "sect", "dom", None),
        P(None, "sect", "dom", None),
        P("sect", "dom", None),
        P("sect", "dom", None, None),
        P("dom", "sect", None),
    )
    out_specs = P(None, "sect", "dom", None)
    return jax.shard_map(shards, mesh=mesh, in_specs=in_specs, out_specs=out_specs, check_vma=False)
```

```python
import math

import jax
import jax.numpy as jnp
import numpy as np
from jax import lax
from jax.experimental import pallas as pl
from jax.experimental.pallas import tpu as pltpu
from jax.sharding import PartitionSpec as P

BLOCK = 128
XROWS = 8
CHUNKS = 2
VMEM = 56 * 1024 * 1024
SPREAD_GROUP = 5
GATHER_GROUP = 5

ewald_beta = 0.1
soft_square = 9.0


def split_table(table):
    table = jnp.asarray(np.asarray(table, np.float32))
    high = table.astype(jnp.bfloat16)
    low = (table - high.astype(jnp.float32)).astype(jnp.bfloat16)
    return high, low


def split(value):
    high = value.astype(jnp.bfloat16)
    low = (value - high.astype(jnp.float32)).astype(jnp.bfloat16)
    return high, low


def dot(left, right, right_dim=0):
    return lax.dot_general(
        left, right, (((1,), (right_dim,)), ((), ())), preferred_element_type=jnp.float32
    )


def dot3(left, right, right_dim=0):
    left = jnp.concatenate([left[0], left[0], left[1]], axis=1)
    right = jnp.concatenate([right[0], right[1], right[0]], axis=right_dim)
    return dot(left, right, right_dim)


def spline(frac):
    inner = 1.0 - frac
    square = frac * frac
    cube = square * frac
    weights = (
        inner * inner * inner / 6.0,
        (3.0 * cube - 6.0 * square + 4.0) / 6.0,
        (-3.0 * cube + 3.0 * square + 3.0 * frac + 1.0) / 6.0,
        cube / 6.0,
    )
    slopes = (
        -inner * inner / 2.0,
        (3.0 * square - 4.0 * frac) / 2.0,
        (-3.0 * square + 2.0 * frac + 1.0) / 2.0,
        square / 2.0,
    )
    return weights, slopes


def turn(steps, mesh_size):
    part = steps * (1.0 / mesh_size)
    part = part - jnp.floor(part)
    half = math.pi * jnp.where(part > 0.5, part - 1.0, part)
    sq = half * half
    sin = half
    cos = jnp.ones_like(half)
    term = half
    for n in range(1, 7):
        term = term * sq * (-1.0 / ((2 * n) * (2 * n + 1)))
        sin = sin + term
    term = cos
    for n in range(1, 8):
        term = term * sq * (-1.0 / ((2 * n - 1) * (2 * n)))
        cos = cos + term
    return 1.0 - 2.0 * sin * sin, 2.0 * sin * cos


def place(offset, values):
    out = jnp.zeros(offset.shape, jnp.float32)
    for k in range(4):
        out = jnp.where(offset == k, values[k], out)
    return out


def pack_kernel(cells, fracs, charges, out):
    rows = [cells[n, 0].astype(jnp.float32) for n in range(3)] + [fracs[n, 0] for n in range(3)]
    atoms = jnp.concatenate(rows + [charges[0], jnp.zeros_like(charges[0])], axis=0)
    for b in range(out.shape[1]):
        part = atoms[:, b * BLOCK : (b + 1) * BLOCK]
        for d in range(out.shape[0]):
            out[d, b] = part


def basis_kernel(which, mesh_size, x_width, z_width, slots_padded, where_ref, blocks, along_x, along_z, high_y, low_y):
    atoms = jnp.concatenate(
        [blocks[d, b] for d in range(blocks.shape[0]) for b in range(blocks.shape[1])], axis=1
    )

    def row(n):
        return atoms[n : n + 1, :]

    lanes = atoms.shape[1]
    charge = row(6)

    def rows(count):
        return lax.broadcasted_iota(jnp.int32, (count, lanes), 0).astype(jnp.float32)

    values = spline(row(3))[which]
    offset = rows(along_x.shape[0]) - (row(0) - (where_ref[0] * x_width).astype(jnp.float32))
    along_x[...] = place(offset, values)
    values = spline(row(4))[which]
    offset = lax.broadcasted_iota(jnp.int32, (mesh_size, lanes), 0) - row(1).astype(jnp.int32)
    high, low = split(place(offset & (mesh_size - 1), values))
    high_y[...] = high
    low_y[...] = low
    values = spline(row(5))[which]
    wave = rows(slots_padded) + (where_ref[1] * z_width).astype(jnp.float32)
    real = jnp.zeros_like(wave)
    imag = jnp.zeros_like(wave)
    cos, sin = turn(wave * row(2), mesh_size)
    by_cos, by_sin = turn(wave[:, 0:128], mesh_size)
    by_cos = jnp.concatenate([by_cos] * (lanes // 128), axis=1)
    by_sin = jnp.concatenate([by_sin] * (lanes // 128), axis=1)
    for k in range(4):
        if k:
            cos, sin = cos * by_cos - sin * by_sin, sin * by_cos + cos * by_sin
        real = real + (charge * values[k]) * cos
        imag = imag - (charge * values[k]) * sin
    along_z[0:slots_padded, :] = real
    along_z[slots_padded:, :] = imag


def groups(count, size):
    return [(low, min(low + size, count)) for low in range(0, count, size)]


def spread_kernel(first, count, slots_padded, wx, zq, bwh, bwl, rh, rl, ih, il, out, *sums):
    step = pl.program_id(0)
    wide = wx[...]
    extent = wide.shape[0]
    right = (bwh[...], bwl[...])

    @pl.when(step == 0)
    def _():
        for acc in sums:
            acc[...] = jnp.zeros_like(acc)

    for low, high in groups(count, SPREAD_GROUP):
        pieces = []
        for c in range(2):
            for g in range(low, high):
                at = c * slots_padded + first + g
                pieces.append(wide * zq[at : at + 1, :])
        part = dot3(split(jnp.concatenate(pieces, axis=0)), right, 1)
        rows = (high - low) * extent
        for c in range(2):
            sums[c][low * extent : high * extent, :] += part[c * rows : (c + 1) * rows]

    @pl.when(step == pl.num_programs(0) - 1)
    def _():
        real, imag = (split(acc[...]) for acc in sums)
        lines = dot3(real, (rh[...], rl[...])) + dot3(imag, (ih[...], il[...]))
        lanes = out.shape[3]
        for s in range(out.shape[0]):
            out[s] = lines[:, s * lanes : (s + 1) * lanes].reshape(out.shape[1:])


def influence_kernel(first, half, scale, where_ref, own, across, edge, flip, same, back, out):
    count, _, lanes = out.shape
    width = own.shape[1]
    lowest = half - max(first + count - 1, 1)
    plain = [own[first + g] for g in range(count) for _ in range(2)]
    plain = split(jnp.concatenate(plain, axis=0))
    pieces = []
    for g in range(count):
        at = half - max(first + g, 1)
        pair = split(across[at - lowest])
        turned = dot(flip[...], pair[0]) + dot(flip[...], pair[1])
        lines = lax.broadcasted_iota(jnp.int32, turned.shape, 0) % width
        pieces.append(jnp.where(lines == 0, edge[at], turned))
    turned = split(jnp.concatenate(pieces, axis=0))
    plain = dot(same[...], plain[0], 1) + dot(same[...], plain[1], 1)
    mirror = dot(back[...], turned[0], 1) + dot(back[...], turned[1], 1)
    for g in range(count):
        keep = scale
        if first + g == half:
            keep = jnp.where(where_ref[2] == 1, scale, 0.0)
        value = plain[:, g * lanes : (g + 1) * lanes]
        if first + g > 0:
            value = value + mirror[:, g * lanes : (g + 1) * lanes]
        out[g] = value * keep


def filter_kernel(lines, factor, th, tl, out):
    sects, count, extent, lanes = lines.shape
    width = extent - XROWS
    mesh_size = sects * width
    table = (th[...], tl[...])
    columns = []
    for g in range(count):
        pieces = []
        for s in range(sects):
            body = lines[s, g]
            before = lines[(s - 1) % sects, g, width:extent, :]
            pieces.append(body[0:XROWS] + before)
            pieces.append(body[XROWS:width])
        columns.append(jnp.concatenate(pieces, axis=0))
    both = dot3(table, split(jnp.concatenate(columns, axis=1)))
    half = lanes // 2
    sign = jnp.where(
        lax.broadcasted_iota(jnp.int32, (mesh_size, lanes), 1) < half, 1.0, -1.0
    )
    columns = []
    for g in range(count):
        cos = both[0:mesh_size, g * lanes : (g + 1) * lanes]
        sin = both[mesh_size:, g * lanes : (g + 1) * lanes]
        columns.append((cos + sign * pltpu.roll(sin, half, 1)) * factor[g])
    both = dot3(table, split(jnp.concatenate(columns, axis=1)))
    for g in range(count):
        cos = both[0:mesh_size, g * lanes : (g + 1) * lanes]
        sin = both[mesh_size:, g * lanes : (g + 1) * lanes]
        field = cos - sign * pltpu.roll(sin, half, 1)
        for s in range(sects):
            after = ((s + 1) % sects) * width
            out[s, g, 0:width, :] = field[s * width : (s + 1) * width]
            out[s, g, width:extent, :] = field[after : after + XROWS]


def gather_kernel(first, count, slots_padded, lines, bh, bl, wx, vx, zq, zv, bwh, bwl, bvh, bvl, *rest):
    *earlier, out, eh, el = rest
    sects, _, extent, lanes = lines.shape
    rows = count * extent
    mesh_size = bwh.shape[0]

    @pl.when(pl.program_id(0) == 0)
    def _():
        joined = jnp.concatenate([lines[s].reshape(rows, lanes) for s in range(sects)], axis=1)
        field = dot3(split(joined), (bh[...], bl[...]))
        pieces = []
        for g in range(count):
            for c in range(2):
                line = field[g * extent : (g + 1) * extent, c * mesh_size : (c + 1) * mesh_size]
                pieces.append(line)
        high, low = split(jnp.concatenate(pieces, axis=0))
        eh[...] = high
        el[...] = low

    weights = (bwh[...], bwl[...])
    slopes = (bvh[...], bvl[...])
    sums = [jnp.zeros(wx.shape, jnp.float32) for _ in range(3)]
    for low, high in groups(count, GATHER_GROUP):
        part = slice(2 * low * extent, 2 * high * extent)
        left = (eh[part, :], el[part, :])
        along = dot3(left, weights)
        slope = dot3(left, slopes)
        for g in range(low, high):
            for c in range(2):
                at = c * slots_padded + first + g
                base = (2 * (g - low) + c) * extent
                line = along[base : base + extent]
                sums[0] = sums[0] + line * zq[at : at + 1, :]
                sums[1] = sums[1] + slope[base : base + extent] * zq[at : at + 1, :]
                sums[2] = sums[2] + line * zv[at : at + 1, :]
    forces = [
        -jnp.sum(total * shape[...], axis=0, keepdims=True)
        for total, shape in zip(sums, (vx, wx, wx))
    ]
    result = jnp.concatenate(forces + [jnp.zeros_like(forces[0])], axis=0)
    width = out.shape[2]
    for d in range(out.shape[0]):
        part = result[:, d * width : (d + 1) * width]
        out[d] = part + earlier[0][d] if earlier else part


def cost(micros):
    return pl.CostEstimate(flops=int(micros * 1.0e9), transcendentals=0, bytes_accessed=int(micros * 1.0e5))


def params():
    return pltpu.CompilerParams(vmem_limit_bytes=VMEM)


def whole(array):
    return pl.BlockSpec(array.shape, lambda *_: (0,) * array.ndim)


def along_atoms(rows, step):
    return pl.BlockSpec((rows, step), lambda n: (0, n))


SMEM = pl.BlockSpec(memory_space=pltpu.SMEM)
IN_VMEM = pl.BlockSpec(memory_space=pltpu.VMEM)


def near_core(array):
    return pltpu.with_memory_space_constraint(array, pltpu.VMEM)


def pair_kernel(centre, others, mesh_size):
    half_mesh = float(mesh_size // 2)
    displace = []
    for component in range(3):
        offset = centre[component][None, :, None] - others[component][:, None, :]
        wrapped = jnp.mod(offset + half_mesh, float(mesh_size)) - half_mesh
        displace.append(
            wrapped + (centre[component + 3][None, :, None] - others[component + 3][:, None, :])
        )
    square = (
        displace[0] * displace[0]
        + displace[1] * displace[1]
        + displace[2] * displace[2]
        + soft_square
    )
    distance = jnp.sqrt(square)
    kernel = (
        lax.erfc(ewald_beta * distance) / (square * distance)
        + 2.0
        * ewald_beta
        / math.sqrt(math.pi)
        * jnp.exp(-ewald_beta * ewald_beta * square)
        / square
    )
    coupling = centre[6][None, :, None] * others[6][:, None, :] * kernel
    return jnp.stack([jnp.sum(coupling * shift_vector, axis=(0, 2)) for shift_vector in displace])


def shards(cells, fracs, charges, pair_blocks, influence):
    sects = lax.axis_size("sect")
    doms = lax.axis_size("dom")
    sect = lax.axis_index("sect")
    dom = lax.axis_index("dom")
    z_width, x_width, mesh_size = influence.shape
    atom_count = charges.shape[2]
    block_count = atom_count // BLOCK
    listed_count = pair_blocks.shape[3]
    half = z_width // 2
    slots = half + 1
    slots_padded = -(-slots // 8) * 8
    extent = x_width + XROWS
    lanes = 2 * x_width
    total = doms * atom_count
    where_am_i = jnp.stack([sect, dom, (dom >= doms // 2).astype(jnp.int32)])

    f32, bf16 = jnp.float32, jnp.bfloat16
    copies = pl.pallas_call(
        pack_kernel,
        out_shape=jax.ShapeDtypeStruct((doms, block_count, 8, BLOCK), f32),
        name="pack",
    )(cells, fracs, charges)
    row = lax.all_to_all(copies, "dom", 0, 0, tiled=True)
    packed = copies[0]

    edges = []
    for s in range(sects):
        for d in range(doms):
            edges.append((s * doms + d, ((sects - s) % sects) * doms + doms - 1 - d))
    flip = np.zeros((2 * x_width, x_width), np.float32)
    for i in range(1, x_width):
        flip[i, x_width - i] = 1.0
        flip[x_width + i, x_width - i] = 1.0
    same = np.eye(mesh_size, dtype=np.float32)
    back = np.roll(same[::-1], 1, axis=0)
    flip, same, back = (jnp.asarray(m).astype(jnp.bfloat16) for m in (flip, same, back))
    firsts = [-(-slots * n // CHUNKS) for n in range(CHUNKS + 1)]
    counts = [b - a for a, b in zip(firsts, firsts[1:])]
    planes = []
    for first, count in zip(firsts, counts):
        lowest = half - max(first + count - 1, 1)
        highest = half - max(first, 1)
        planes.append(influence[half + lowest : half + highest + 1])
    sect_flip = [(s, sects - 1 - s) for s in range(sects)]
    dom_flip = [(d, doms - 1 - d) for d in range(doms)]
    planes = [lax.ppermute(p, "sect", sect_flip) for p in planes]

    step = np.arange(mesh_size)
    angle = 2.0 * np.pi * (np.outer(step, step) % mesh_size) / mesh_size
    cos, sin = np.cos(angle), np.sin(angle)

    def by_sect(real, imag):
        real = real.reshape(mesh_size, sects, 1, x_width)
        imag = imag.reshape(mesh_size, sects, 1, x_width)
        return np.concatenate([real, imag], axis=2).reshape(mesh_size, 2 * mesh_size)

    rh, rl = split_table(by_sect(cos, -sin))
    ih, il = split_table(by_sect(sin, cos))
    bh, bl = split_table(np.concatenate([by_sect(cos, -sin).T, by_sect(sin, cos).T], axis=1))
    th, tl = split_table(np.concatenate([cos, sin], axis=0))

    atom_step = 512
    grid = (total // atom_step,)
    shapes = [
        ((extent, total), f32),
        ((2 * slots_padded, total), f32),
        ((mesh_size, total), bf16),
        ((mesh_size, total), bf16),
    ]

    def basis(which, blocks):
        return pl.pallas_call(
            lambda *refs: basis_kernel(which, mesh_size, x_width, z_width, slots_padded, *refs),
            grid=grid,
            in_specs=[
                SMEM,
                pl.BlockSpec(
                    (atom_step // atom_count, block_count, 8, BLOCK), lambda n: (n, 0, 0, 0)
                ),
            ],
            out_specs=[along_atoms(shape[0], atom_step) for shape, _ in shapes],
            out_shape=[jax.ShapeDtypeStruct(shape, dtype) for shape, dtype in shapes],
            compiler_params=params(),
            cost_estimate=cost(4),
            name="basis",
        )(where_am_i, blocks)

    wx, zq, bwh, bwl = basis(0, row)

    sent = []
    for first, count in zip(firsts, counts):
        shape = (sects, count, extent, lanes)
        lines = pl.pallas_call(
            lambda *refs, first=first, count=count: spread_kernel(first, count, slots_padded, *refs),
            grid=grid,
            in_specs=[
                along_atoms(extent, atom_step),
                along_atoms(2 * slots_padded, atom_step),
                along_atoms(mesh_size, atom_step),
                along_atoms(mesh_size, atom_step),
            ]
            + [whole(t) for t in (rh, rl, ih, il)],
            out_specs=pl.BlockSpec(shape, lambda n: (0, 0, 0, 0)),
            out_shape=jax.ShapeDtypeStruct(shape, f32),
            scratch_shapes=[pltpu.VMEM((count * extent, mesh_size), f32)] * 2,
            compiler_params=params(),
            cost_estimate=cost(9),
            name="spread",
        )(wx, zq, bwh, bwl, rh, rl, ih, il)
        sent.append(lines)
    corner, beside, planes[0], sent[0] = lax.optimization_barrier(
        (influence[half:, 0:1], row, planes[0], sent[0])
    )
    vx, zv, bvh, bvl = basis(1, beside)
    planes[0] = lax.ppermute(planes[0], "dom", dom_flip)
    edge = lax.ppermute(corner, ("sect", "dom"), edges)
    sent = [lax.all_to_all(lines, "sect", split_axis=0, concat_axis=0, tiled=True) for lines in sent]
    planes[1:], beside, sent[0] = lax.optimization_barrier((planes[1:], beside, sent[0]))
    planes[1:] = [lax.ppermute(p, "dom", dom_flip) for p in planes[1:]]
    planes[0], edge, sent[0] = lax.optimization_barrier((planes[0], edge, sent[0]))
    ahead = [(s, (s + 1) % sects) for s in range(sects)]
    behind = [(b, a) for a, b in ahead]
    near = [lax.ppermute(beside, "sect", ahead), lax.ppermute(beside, "sect", behind)]

    def folded(first, count, mirror):
        return pl.pallas_call(
            lambda *refs: influence_kernel(first, half, float(mesh_size) ** -3, *refs),
            in_specs=[SMEM] + [pl.BlockSpec(memory_space=pltpu.VMEM)] * 6,
            out_specs=pl.BlockSpec(memory_space=pltpu.VMEM),
            out_shape=jax.ShapeDtypeStruct((count, mesh_size, lanes), f32),
            compiler_params=params(),
            cost_estimate=cost(3.5),
            name="influence",
        )(where_am_i, influence, mirror, near_core(edge), flip, same, back)

    factors = [folded(firsts[0], counts[0], planes[0])]
    for n in range(1, CHUNKS):
        factors.append(folded(firsts[n], counts[n], planes[n]))
    fields = []
    near, row, packed, sent[-1] = lax.optimization_barrier((near, row, packed, sent[-1]))
    for lines, factor in zip(sent, factors):
        field = pl.pallas_call(
            filter_kernel,
            grid=(1,),
            in_specs=[
                IN_VMEM,
                IN_VMEM,
                whole(th),
                whole(tl),
            ],
            out_specs=whole(lines),
            out_shape=jax.ShapeDtypeStruct(lines.shape, f32),
            compiler_params=params(),
            cost_estimate=cost(5.5),
            name="filter",
        )(near_core(lines), factor, th, tl)
        fields.append(field)
    fields = [lax.all_to_all(field, "sect", split_axis=0, concat_axis=0, tiled=True) for field in fields]

    listed = pair_blocks[0, 0]
    neighbour = listed // block_count
    near = jnp.stack([near[0], row, near[1]])
    from_dom = (dom + neighbour % 3 - 1) % doms
    source = (neighbour // 3 * doms + from_dom) * block_count + listed % block_count
    pool = near.reshape(3 * doms * block_count, 8 * BLOCK)
    pick = (source.reshape(-1, 1) == jnp.arange(pool.shape[0], dtype=jnp.int32)[None]).astype(f32)
    chosen = lax.dot_general(
        pick, pool, (((1,), (0,)), ((), ())), precision=lax.Precision.HIGHEST, preferred_element_type=f32
    ).reshape(block_count, listed_count, 8, BLOCK)
    chosen = jnp.transpose(chosen, (0, 2, 1, 3))
    block_forces = jnp.stack(
        [pair_kernel(packed[b], chosen[b], mesh_size) for b in range(block_count)], axis=1
    )
    short_force = block_forces.reshape(3, atom_count)

    earlier = []
    by_dom = pl.BlockSpec((atom_step // atom_count, 4, atom_count), lambda n: (n, 0, 0))
    for lines, first, count in zip(fields, firsts, counts):
        earlier = [pl.pallas_call(
            lambda *refs, first=first, count=count: gather_kernel(first, count, slots_padded, *refs),
            grid=grid,
            in_specs=[IN_VMEM, whole(bh), whole(bl)]
            + [along_atoms(a.shape[0], atom_step) for a in (wx, vx, zq, zv, bwh, bwl, bvh, bvl)]
            + [by_dom] * len(earlier),
            out_specs=by_dom,
            out_shape=jax.ShapeDtypeStruct((doms, 4, atom_count), f32),
            scratch_shapes=[pltpu.VMEM((2 * count * extent, mesh_size), bf16)] * 2,
            compiler_params=params(),
            cost_estimate=cost(13),
            name="gather",
        )(near_core(lines), bh, bl, wx, vx, zq, zv, bwh, bwl, bvh, bvl, *earlier)]
    shares = lax.all_to_all(earlier[0], "dom", 0, 0, tiled=True)
    mesh_force = jnp.sum(shares, axis=0)[:3]
    return (short_force + mesh_force).reshape(3, 1, 1, atom_count)


def solution(mesh):
    in_specs = (
        P(None, "sect", "dom", None),
        P(None, "sect", "dom", None),
        P("sect", "dom", None),
        P("sect", "dom", None, None),
        P("dom", "sect", None),
    )
    out_specs = P(None, "sect", "dom", None)
    return jax.shard_map(shards, mesh=mesh, in_specs=in_specs, out_specs=out_specs, check_vma=False)
```

```python
import math

import jax
import jax.numpy as jnp
import numpy as np
from jax import lax
from jax.experimental import pallas as pl
from jax.experimental.pallas import tpu as pltpu
from jax.sharding import PartitionSpec as P

BLOCK = 128
XROWS = 8
CHUNKS = 2
VMEM = 56 * 1024 * 1024
SPREAD_GROUP = 5
GATHER_GROUP = 5

ewald_beta = 0.1
soft_square = 9.0


def split_table(table):
    table = jnp.asarray(np.asarray(table, np.float32))
    high = table.astype(jnp.bfloat16)
    low = (table - high.astype(jnp.float32)).astype(jnp.bfloat16)
    return high, low


def split(value):
    high = value.astype(jnp.bfloat16)
    low = (value - high.astype(jnp.float32)).astype(jnp.bfloat16)
    return high, low


def dot(left, right, right_dim=0):
    return lax.dot_general(
        left, right, (((1,), (right_dim,)), ((), ())), preferred_element_type=jnp.float32
    )


def dot3(left, right, right_dim=0):
    left = jnp.concatenate([left[0], left[0], left[1]], axis=1)
    right = jnp.concatenate([right[0], right[1], right[0]], axis=right_dim)
    return dot(left, right, right_dim)


def spline(frac):
    inner = 1.0 - frac
    square = frac * frac
    cube = square * frac
    weights = (
        inner * inner * inner / 6.0,
        (3.0 * cube - 6.0 * square + 4.0) / 6.0,
        (-3.0 * cube + 3.0 * square + 3.0 * frac + 1.0) / 6.0,
        cube / 6.0,
    )
    slopes = (
        -inner * inner / 2.0,
        (3.0 * square - 4.0 * frac) / 2.0,
        (-3.0 * square + 2.0 * frac + 1.0) / 2.0,
        square / 2.0,
    )
    return weights, slopes


def turn(steps, mesh_size):
    part = steps * (1.0 / mesh_size)
    part = part - jnp.floor(part)
    half = math.pi * jnp.where(part > 0.5, part - 1.0, part)
    sq = half * half
    sin = half
    cos = jnp.ones_like(half)
    term = half
    for n in range(1, 7):
        term = term * sq * (-1.0 / ((2 * n) * (2 * n + 1)))
        sin = sin + term
    term = cos
    for n in range(1, 8):
        term = term * sq * (-1.0 / ((2 * n - 1) * (2 * n)))
        cos = cos + term
    return 1.0 - 2.0 * sin * sin, 2.0 * sin * cos


def place(offset, values):
    out = jnp.zeros(offset.shape, jnp.float32)
    for k in range(4):
        out = jnp.where(offset == k, values[k], out)
    return out


def pack_kernel(cells, fracs, charges, out):
    rows = [cells[n, 0].astype(jnp.float32) for n in range(3)] + [fracs[n, 0] for n in range(3)]
    atoms = jnp.concatenate(rows + [charges[0], jnp.zeros_like(charges[0])], axis=0)
    for b in range(out.shape[1]):
        part = atoms[:, b * BLOCK : (b + 1) * BLOCK]
        for d in range(out.shape[0]):
            out[d, b] = part


def basis_kernel(which, mesh_size, x_width, z_width, slots_padded, where_ref, blocks, along_x, along_z, high_y, low_y):
    atoms = jnp.concatenate(
        [blocks[d, b] for d in range(blocks.shape[0]) for b in range(blocks.shape[1])], axis=1
    )

    def row(n):
        return atoms[n : n + 1, :]

    lanes = atoms.shape[1]
    charge = row(6)

    def rows(count):
        return lax.broadcasted_iota(jnp.int32, (count, lanes), 0).astype(jnp.float32)

    values = spline(row(3))[which]
    offset = rows(along_x.shape[0]) - (row(0) - (where_ref[0] * x_width).astype(jnp.float32))
    along_x[...] = place(offset, values)
    values = spline(row(4))[which]
    offset = lax.broadcasted_iota(jnp.int32, (mesh_size, lanes), 0) - row(1).astype(jnp.int32)
    high, low = split(place(offset & (mesh_size - 1), values))
    high_y[...] = high
    low_y[...] = low
    values = spline(row(5))[which]
    wave = rows(slots_padded) + (where_ref[1] * z_width).astype(jnp.float32)
    real = jnp.zeros_like(wave)
    imag = jnp.zeros_like(wave)
    cos, sin = turn(wave * row(2), mesh_size)
    by_cos, by_sin = turn(wave[:, 0:128], mesh_size)
    by_cos = jnp.concatenate([by_cos] * (lanes // 128), axis=1)
    by_sin = jnp.concatenate([by_sin] * (lanes // 128), axis=1)
    for k in range(4):
        if k:
            cos, sin = cos * by_cos - sin * by_sin, sin * by_cos + cos * by_sin
        real = real + (charge * values[k]) * cos
        imag = imag - (charge * values[k]) * sin
    along_z[0:slots_padded, :] = real
    along_z[slots_padded:, :] = imag


def groups(count, size):
    return [(low, min(low + size, count)) for low in range(0, count, size)]


def spread_kernel(first, count, slots_padded, wx, zq, bwh, bwl, rh, rl, ih, il, out, *sums):
    step = pl.program_id(0)
    wide = wx[...]
    extent = wide.shape[0]
    right = (bwh[...], bwl[...])

    @pl.when(step == 0)
    def _():
        for acc in sums:
            acc[...] = jnp.zeros_like(acc)

    for low, high in groups(count, SPREAD_GROUP):
        pieces = []
        for c in range(2):
            for g in range(low, high):
                at = c * slots_padded + first + g
                pieces.append(wide * zq[at : at + 1, :])
        part = dot3(split(jnp.concatenate(pieces, axis=0)), right, 1)
        rows = (high - low) * extent
        for c in range(2):
            sums[c][low * extent : high * extent, :] += part[c * rows : (c + 1) * rows]

    @pl.when(step == pl.num_programs(0) - 1)
    def _():
        real, imag = (split(acc[...]) for acc in sums)
        lines = dot3(real, (rh[...], rl[...])) + dot3(imag, (ih[...], il[...]))
        lanes = out.shape[3]
        for s in range(out.shape[0]):
            out[s] = lines[:, s * lanes : (s + 1) * lanes].reshape(out.shape[1:])


def influence_kernel(first, half, scale, where_ref, own, across, edge, flip, same, back, out):
    count, _, lanes = out.shape
    width = own.shape[1]
    lowest = half - max(first + count - 1, 1)
    both_flip = jnp.concatenate([flip[...]] * 2, axis=1)
    mirror = []
    for g in range(count):
        at = half - max(first + g, 1)
        pair = jnp.concatenate(split(across[at - lowest]), axis=0)
        turned = dot(both_flip, pair)
        lines = lax.broadcasted_iota(jnp.int32, turned.shape, 0) % width
        turned = jnp.where(lines == 0, edge[at], turned)
        mirror.append(turned if first + g > 0 else jnp.zeros_like(turned))
    plain = [own[first + g] for g in range(count) for _ in range(2)]
    plain = split(jnp.concatenate(plain, axis=0))
    mirror = split(jnp.concatenate(mirror, axis=0))
    left = jnp.concatenate([same[...]] * 2 + [back[...]] * 2, axis=1)
    values = dot(left, jnp.concatenate(plain + mirror, axis=1), 1)
    for g in range(count):
        keep = scale
        if first + g == half:
            keep = jnp.where(where_ref[2] == 1, scale, 0.0)
        out[g] = values[:, g * lanes : (g + 1) * lanes] * keep


def filter_kernel(lines, factor, th, tl, out):
    sects, count, extent, lanes = lines.shape
    width = extent - XROWS
    mesh_size = sects * width
    table = (th[...], tl[...])
    columns = []
    for g in range(count):
        pieces = []
        for s in range(sects):
            body = lines[s, g]
            before = lines[(s - 1) % sects, g, width:extent, :]
            pieces.append(body[0:XROWS] + before)
            pieces.append(body[XROWS:width])
        columns.append(jnp.concatenate(pieces, axis=0))
    both = dot3(table, split(jnp.concatenate(columns, axis=1)))
    half = lanes // 2
    sign = jnp.where(
        lax.broadcasted_iota(jnp.int32, (mesh_size, lanes), 1) < half, 1.0, -1.0
    )
    columns = []
    for g in range(count):
        cos = both[0:mesh_size, g * lanes : (g + 1) * lanes]
        sin = both[mesh_size:, g * lanes : (g + 1) * lanes]
        columns.append((cos + sign * pltpu.roll(sin, half, 1)) * factor[g])
    both = dot3(table, split(jnp.concatenate(columns, axis=1)))
    for g in range(count):
        cos = both[0:mesh_size, g * lanes : (g + 1) * lanes]
        sin = both[mesh_size:, g * lanes : (g + 1) * lanes]
        field = cos - sign * pltpu.roll(sin, half, 1)
        for s in range(sects):
            after = ((s + 1) % sects) * width
            out[s, g, 0:width, :] = field[s * width : (s + 1) * width]
            out[s, g, width:extent, :] = field[after : after + XROWS]


def gather_kernel(first, count, slots_padded, lines, bh, bl, wx, vx, zq, zv, bwh, bwl, bvh, bvl, *rest):
    *earlier, out, eh, el = rest
    sects, _, extent, lanes = lines.shape
    rows = count * extent
    mesh_size = bwh.shape[0]

    @pl.when(pl.program_id(0) == 0)
    def _():
        joined = jnp.concatenate([lines[s].reshape(rows, lanes) for s in range(sects)], axis=1)
        field = dot3(split(joined), (bh[...], bl[...]))
        pieces = []
        for g in range(count):
            for c in range(2):
                line = field[g * extent : (g + 1) * extent, c * mesh_size : (c + 1) * mesh_size]
                pieces.append(line)
        high, low = split(jnp.concatenate(pieces, axis=0))
        eh[...] = high
        el[...] = low

    weights = (bwh[...], bwl[...])
    slopes = (bvh[...], bvl[...])
    sums = [jnp.zeros(wx.shape, jnp.float32) for _ in range(3)]
    for low, high in groups(count, GATHER_GROUP):
        part = slice(2 * low * extent, 2 * high * extent)
        left = (eh[part, :], el[part, :])
        along = dot3(left, weights)
        slope = dot3(left, slopes)
        for g in range(low, high):
            for c in range(2):
                at = c * slots_padded + first + g
                base = (2 * (g - low) + c) * extent
                line = along[base : base + extent]
                sums[0] = sums[0] + line * zq[at : at + 1, :]
                sums[1] = sums[1] + slope[base : base + extent] * zq[at : at + 1, :]
                sums[2] = sums[2] + line * zv[at : at + 1, :]
    forces = [
        -jnp.sum(total * shape[...], axis=0, keepdims=True)
        for total, shape in zip(sums, (vx, wx, wx))
    ]
    result = jnp.concatenate(forces + [jnp.zeros_like(forces[0])], axis=0)
    width = out.shape[2]
    for d in range(out.shape[0]):
        part = result[:, d * width : (d + 1) * width]
        out[d] = part + earlier[0][d] if earlier else part


def cost(micros):
    return pl.CostEstimate(flops=int(micros * 1.0e9), transcendentals=0, bytes_accessed=int(micros * 1.0e5))


def params():
    return pltpu.CompilerParams(vmem_limit_bytes=VMEM)


def whole(array):
    return pl.BlockSpec(array.shape, lambda *_: (0,) * array.ndim)


def along_atoms(rows, step):
    return pl.BlockSpec((rows, step), lambda n: (0, n))


SMEM = pl.BlockSpec(memory_space=pltpu.SMEM)
IN_VMEM = pl.BlockSpec(memory_space=pltpu.VMEM)


def near_core(array):
    return pltpu.with_memory_space_constraint(array, pltpu.VMEM)


def pair_kernel(centre, others, mesh_size):
    half_mesh = float(mesh_size // 2)
    displace = []
    for component in range(3):
        offset = centre[component][None, :, None] - others[component][:, None, :]
        wrapped = jnp.mod(offset + half_mesh, float(mesh_size)) - half_mesh
        displace.append(
            wrapped + (centre[component + 3][None, :, None] - others[component + 3][:, None, :])
        )
    square = (
        displace[0] * displace[0]
        + displace[1] * displace[1]
        + displace[2] * displace[2]
        + soft_square
    )
    distance = jnp.sqrt(square)
    kernel = (
        lax.erfc(ewald_beta * distance) / (square * distance)
        + 2.0
        * ewald_beta
        / math.sqrt(math.pi)
        * jnp.exp(-ewald_beta * ewald_beta * square)
        / square
    )
    coupling = centre[6][None, :, None] * others[6][:, None, :] * kernel
    return jnp.stack([jnp.sum(coupling * shift_vector, axis=(0, 2)) for shift_vector in displace])


def shards(cells, fracs, charges, pair_blocks, influence):
    sects = lax.axis_size("sect")
    doms = lax.axis_size("dom")
    sect = lax.axis_index("sect")
    dom = lax.axis_index("dom")
    z_width, x_width, mesh_size = influence.shape
    atom_count = charges.shape[2]
    block_count = atom_count // BLOCK
    listed_count = pair_blocks.shape[3]
    half = z_width // 2
    slots = half + 1
    slots_padded = -(-slots // 8) * 8
    extent = x_width + XROWS
    lanes = 2 * x_width
    total = doms * atom_count
    where_am_i = jnp.stack([sect, dom, (dom >= doms // 2).astype(jnp.int32)])

    f32, bf16 = jnp.float32, jnp.bfloat16
    copies = pl.pallas_call(
        pack_kernel,
        out_shape=jax.ShapeDtypeStruct((doms, block_count, 8, BLOCK), f32),
        name="pack",
    )(cells, fracs, charges)
    row = lax.all_to_all(copies, "dom", 0, 0, tiled=True)
    packed = copies[0]

    edges = []
    for s in range(sects):
        for d in range(doms):
            edges.append((s * doms + d, ((sects - s) % sects) * doms + doms - 1 - d))
    flip = np.zeros((2 * x_width, x_width), np.float32)
    for i in range(1, x_width):
        flip[i, x_width - i] = 1.0
        flip[x_width + i, x_width - i] = 1.0
    same = np.eye(mesh_size, dtype=np.float32)
    back = np.roll(same[::-1], 1, axis=0)
    flip, same, back = (jnp.asarray(m).astype(jnp.bfloat16) for m in (flip, same, back))
    firsts = [-(-slots * n // CHUNKS) for n in range(CHUNKS + 1)]
    counts = [b - a for a, b in zip(firsts, firsts[1:])]
    planes = []
    for first, count in zip(firsts, counts):
        lowest = half - max(first + count - 1, 1)
        highest = half - max(first, 1)
        planes.append(influence[half + lowest : half + highest + 1])
    sect_flip = [(s, sects - 1 - s) for s in range(sects)]
    dom_flip = [(d, doms - 1 - d) for d in range(doms)]
    planes = [lax.ppermute(p, "sect", sect_flip) for p in planes]

    step = np.arange(mesh_size)
    angle = 2.0 * np.pi * (np.outer(step, step) % mesh_size) / mesh_size
    cos, sin = np.cos(angle), np.sin(angle)

    def by_sect(real, imag):
        real = real.reshape(mesh_size, sects, 1, x_width)
        imag = imag.reshape(mesh_size, sects, 1, x_width)
        return np.concatenate([real, imag], axis=2).reshape(mesh_size, 2 * mesh_size)

    rh, rl = split_table(by_sect(cos, -sin))
    ih, il = split_table(by_sect(sin, cos))
    bh, bl = split_table(np.concatenate([by_sect(cos, -sin).T, by_sect(sin, cos).T], axis=1))
    th, tl = split_table(np.concatenate([cos, sin], axis=0))

    atom_step = 512
    grid = (total // atom_step,)
    shapes = [
        ((extent, total), f32),
        ((2 * slots_padded, total), f32),
        ((mesh_size, total), bf16),
        ((mesh_size, total), bf16),
    ]

    def basis(which, blocks):
        return pl.pallas_call(
            lambda *refs: basis_kernel(which, mesh_size, x_width, z_width, slots_padded, *refs),
            grid=grid,
            in_specs=[
                SMEM,
                pl.BlockSpec(
                    (atom_step // atom_count, block_count, 8, BLOCK), lambda n: (n, 0, 0, 0)
                ),
            ],
            out_specs=[along_atoms(shape[0], atom_step) for shape, _ in shapes],
            out_shape=[jax.ShapeDtypeStruct(shape, dtype) for shape, dtype in shapes],
            compiler_params=params(),
            cost_estimate=cost(0.1 if which else 4),
            name="basis",
        )(where_am_i, blocks)

    wx, zq, bwh, bwl = basis(0, row)

    sent = []
    for first, count in zip(firsts, counts):
        shape = (sects, count, extent, lanes)
        lines = pl.pallas_call(
            lambda *refs, first=first, count=count: spread_kernel(first, count, slots_padded, *refs),
            grid=grid,
            in_specs=[
                along_atoms(extent, atom_step),
                along_atoms(2 * slots_padded, atom_step),
                along_atoms(mesh_size, atom_step),
                along_atoms(mesh_size, atom_step),
            ]
            + [whole(t) for t in (rh, rl, ih, il)],
            out_specs=pl.BlockSpec(shape, lambda n: (0, 0, 0, 0)),
            out_shape=jax.ShapeDtypeStruct(shape, f32),
            scratch_shapes=[pltpu.VMEM((count * extent, mesh_size), f32)] * 2,
            compiler_params=params(),
            cost_estimate=cost(9),
            name="spread",
        )(wx, zq, bwh, bwl, rh, rl, ih, il)
        sent.append(lines)
    corner, beside, planes[0], sent[0] = lax.optimization_barrier(
        (influence[half:, 0:1], row, planes[0], sent[0])
    )
    vx, zv, bvh, bvl = basis(1, beside)
    vx, sent[-1] = lax.optimization_barrier((vx, sent[-1]))
    planes[0] = lax.ppermute(planes[0], "dom", dom_flip)
    edge = lax.ppermute(corner, ("sect", "dom"), edges)
    sent = [lax.all_to_all(lines, "sect", split_axis=0, concat_axis=0, tiled=True) for lines in sent]
    planes[1:], beside, sent[0] = lax.optimization_barrier((planes[1:], beside, sent[0]))
    planes[1:] = [lax.ppermute(p, "dom", dom_flip) for p in planes[1:]]
    planes[0], edge, sent[0] = lax.optimization_barrier((planes[0], edge, sent[0]))
    ahead = [(s, (s + 1) % sects) for s in range(sects)]
    behind = [(b, a) for a, b in ahead]
    near = [lax.ppermute(beside, "sect", ahead), lax.ppermute(beside, "sect", behind)]

    def folded(first, count, mirror):
        return pl.pallas_call(
            lambda *refs: influence_kernel(first, half, float(mesh_size) ** -3, *refs),
            in_specs=[SMEM] + [pl.BlockSpec(memory_space=pltpu.VMEM)] * 6,
            out_specs=pl.BlockSpec(memory_space=pltpu.VMEM),
            out_shape=jax.ShapeDtypeStruct((count, mesh_size, lanes), f32),
            compiler_params=params(),
            cost_estimate=cost(3.5),
            name="influence",
        )(where_am_i, influence, mirror, near_core(edge), flip, same, back)

    factors = [folded(firsts[0], counts[0], planes[0])]
    for n in range(1, CHUNKS):
        factors.append(folded(firsts[n], counts[n], planes[n]))
    fields = []
    near, row, packed, sent[-1] = lax.optimization_barrier((near, row, packed, sent[-1]))
    for lines, factor in zip(sent, factors):
        field = pl.pallas_call(
            filter_kernel,
            grid=(1,),
            in_specs=[
                IN_VMEM,
                IN_VMEM,
                whole(th),
                whole(tl),
            ],
            out_specs=whole(lines),
            out_shape=jax.ShapeDtypeStruct(lines.shape, f32),
            compiler_params=params(),
            cost_estimate=cost(5.5),
            name="filter",
        )(near_core(lines), factor, th, tl)
        fields.append(field)
    fields = [lax.all_to_all(field, "sect", split_axis=0, concat_axis=0, tiled=True) for field in fields]

    listed = pair_blocks[0, 0]
    neighbour = listed // block_count
    near = jnp.stack([near[0], row, near[1]])
    from_dom = (dom + neighbour % 3 - 1) % doms
    source = (neighbour // 3 * doms + from_dom) * block_count + listed % block_count
    pool = near.reshape(3 * doms * block_count, 8 * BLOCK)
    pick = (source.reshape(-1, 1) == jnp.arange(pool.shape[0], dtype=jnp.int32)[None]).astype(f32)
    chosen = lax.dot_general(
        pick, pool, (((1,), (0,)), ((), ())), precision=lax.Precision.HIGHEST, preferred_element_type=f32
    ).reshape(block_count, listed_count, 8, BLOCK)
    chosen = jnp.transpose(chosen, (0, 2, 1, 3))
    block_forces = jnp.stack(
        [pair_kernel(packed[b], chosen[b], mesh_size) for b in range(block_count)], axis=1
    )
    short_force = block_forces.reshape(3, atom_count)

    earlier = []
    by_dom = pl.BlockSpec((atom_step // atom_count, 4, atom_count), lambda n: (n, 0, 0))
    for lines, first, count in zip(fields, firsts, counts):
        earlier = [pl.pallas_call(
            lambda *refs, first=first, count=count: gather_kernel(first, count, slots_padded, *refs),
            grid=grid,
            in_specs=[IN_VMEM, whole(bh), whole(bl)]
            + [along_atoms(a.shape[0], atom_step) for a in (wx, vx, zq, zv, bwh, bwl, bvh, bvl)]
            + [by_dom] * len(earlier),
            out_specs=by_dom,
            out_shape=jax.ShapeDtypeStruct((doms, 4, atom_count), f32),
            scratch_shapes=[pltpu.VMEM((2 * count * extent, mesh_size), bf16)] * 2,
            compiler_params=params(),
            cost_estimate=cost(13),
            name="gather",
        )(near_core(lines), bh, bl, wx, vx, zq, zv, bwh, bwl, bvh, bvl, *earlier)]
    shares = lax.all_to_all(earlier[0], "dom", 0, 0, tiled=True)
    mesh_force = jnp.sum(shares, axis=0)[:3]
    return (short_force + mesh_force).reshape(3, 1, 1, atom_count)


def solution(mesh):
    in_specs = (
        P(None, "sect", "dom", None),
        P(None, "sect", "dom", None),
        P("sect", "dom", None),
        P("sect", "dom", None, None),
        P("dom", "sect", None),
    )
    out_specs = P(None, "sect", "dom", None)
    return jax.shard_map(shards, mesh=mesh, in_specs=in_specs, out_specs=out_specs, check_vma=False)
```

```python
import math

import jax
import jax.numpy as jnp
import numpy as np
from jax import lax
from jax.experimental import pallas as pl
from jax.experimental.pallas import tpu as pltpu
from jax.sharding import PartitionSpec as P

BLOCK = 128
PAST = 3
CHUNKS = 2
VMEM = 56 * 1024 * 1024
SPREAD_GROUP = 5
GATHER_GROUP = 5

ewald_beta = 0.1
soft_square = 9.0


def split_table(table):
    table = jnp.asarray(np.asarray(table, np.float32))
    high = table.astype(jnp.bfloat16)
    low = (table - high.astype(jnp.float32)).astype(jnp.bfloat16)
    return high, low


def split(value):
    high = value.astype(jnp.bfloat16)
    low = (value - high.astype(jnp.float32)).astype(jnp.bfloat16)
    return high, low


def dot(left, right, right_dim=0):
    return lax.dot_general(
        left, right, (((1,), (right_dim,)), ((), ())), preferred_element_type=jnp.float32
    )


def dot3(left, right, right_dim=0):
    left = jnp.concatenate([left[0], left[0], left[1]], axis=1)
    right = jnp.concatenate([right[0], right[1], right[0]], axis=right_dim)
    return dot(left, right, right_dim)


def spline(frac):
    inner = 1.0 - frac
    square = frac * frac
    cube = square * frac
    weights = (
        inner * inner * inner / 6.0,
        (3.0 * cube - 6.0 * square + 4.0) / 6.0,
        (-3.0 * cube + 3.0 * square + 3.0 * frac + 1.0) / 6.0,
        cube / 6.0,
    )
    slopes = (
        -inner * inner / 2.0,
        (3.0 * square - 4.0 * frac) / 2.0,
        (-3.0 * square + 2.0 * frac + 1.0) / 2.0,
        square / 2.0,
    )
    return weights, slopes


def turn(steps, mesh_size):
    part = steps * (1.0 / mesh_size)
    part = part - jnp.floor(part)
    half = math.pi * jnp.where(part > 0.5, part - 1.0, part)
    sq = half * half
    sin = half
    cos = jnp.ones_like(half)
    term = half
    for n in range(1, 7):
        term = term * sq * (-1.0 / ((2 * n) * (2 * n + 1)))
        sin = sin + term
    term = cos
    for n in range(1, 8):
        term = term * sq * (-1.0 / ((2 * n - 1) * (2 * n)))
        cos = cos + term
    return 1.0 - 2.0 * sin * sin, 2.0 * sin * cos


def place(offset, values):
    out = jnp.zeros(offset.shape, jnp.float32)
    for k in range(4):
        out = jnp.where(offset == k, values[k], out)
    return out


def pack_kernel(cells, fracs, charges, out):
    rows = [cells[n, 0].astype(jnp.float32) for n in range(3)] + [fracs[n, 0] for n in range(3)]
    atoms = jnp.concatenate(rows + [charges[0], jnp.zeros_like(charges[0])], axis=0)
    for b in range(out.shape[1]):
        part = atoms[:, b * BLOCK : (b + 1) * BLOCK]
        for d in range(out.shape[0]):
            out[d, b] = part


def basis_kernel(which, mesh_size, x_width, z_width, slots_padded, where_ref, blocks, along_x, along_z, high_y, low_y):
    atoms = jnp.concatenate(
        [blocks[d, b] for d in range(blocks.shape[0]) for b in range(blocks.shape[1])], axis=1
    )

    def row(n):
        return atoms[n : n + 1, :]

    lanes = atoms.shape[1]
    charge = row(6)

    def rows(count):
        return lax.broadcasted_iota(jnp.int32, (count, lanes), 0).astype(jnp.float32)

    values = spline(row(3))[which]
    offset = rows(along_x.shape[0]) - (row(0) - (where_ref[0] * x_width).astype(jnp.float32))
    along_x[...] = place(offset, values)
    values = spline(row(4))[which]
    offset = lax.broadcasted_iota(jnp.int32, (mesh_size, lanes), 0) - row(1).astype(jnp.int32)
    high, low = split(place(offset & (mesh_size - 1), values))
    high_y[...] = high
    low_y[...] = low
    values = spline(row(5))[which]
    wave = rows(slots_padded) + (where_ref[1] * z_width).astype(jnp.float32)
    real = jnp.zeros_like(wave)
    imag = jnp.zeros_like(wave)
    cos, sin = turn(wave * row(2), mesh_size)
    by_cos, by_sin = turn(wave[:, 0:128], mesh_size)
    by_cos = jnp.concatenate([by_cos] * (lanes // 128), axis=1)
    by_sin = jnp.concatenate([by_sin] * (lanes // 128), axis=1)
    for k in range(4):
        if k:
            cos, sin = cos * by_cos - sin * by_sin, sin * by_cos + cos * by_sin
        real = real + (charge * values[k]) * cos
        imag = imag - (charge * values[k]) * sin
    along_z[0:slots_padded, :] = real
    along_z[slots_padded:, :] = imag


def groups(count, size):
    return [(low, min(low + size, count)) for low in range(0, count, size)]


def spread_kernel(first, count, slots_padded, wx, zq, bwh, bwl, rh, rl, ih, il, out, *sums):
    step = pl.program_id(0)
    padded = -(-count // 8) * 8
    width = sums[0].shape[0] - PAST * padded
    width = width // count
    wide = wx[0:width, :]
    right = (bwh[...], bwl[...])

    @pl.when(step == 0)
    def _():
        for acc in sums:
            acc[...] = jnp.zeros_like(acc)

    for low, high in groups(count, SPREAD_GROUP):
        pieces = []
        for c in range(2):
            base = c * slots_padded + first
            pieces += [wide * zq[base + g : base + g + 1, :] for g in range(low, high)]
            if high == count:
                strip = zq[base : base + padded, :]
                pieces += [wx[width + i : width + i + 1, :] * strip for i in range(PAST)]
        part = dot3(split(jnp.concatenate(pieces, axis=0)), right, 1)
        rows = part.shape[0] // 2
        for c in range(2):
            sums[c][low * width : low * width + rows, :] += part[c * rows : (c + 1) * rows]

    @pl.when(step == pl.num_programs(0) - 1)
    def _():
        real, imag = (split(acc[...]) for acc in sums)
        lines = dot3(real, (rh[...], rl[...])) + dot3(imag, (ih[...], il[...]))
        lanes = out.shape[2]
        for s in range(out.shape[0]):
            out[s] = lines[:, s * lanes : (s + 1) * lanes]


def influence_kernel(first, half, scale, where_ref, own, across, edge, flip, same, back, out):
    count, _, lanes = out.shape
    width = own.shape[1]
    lowest = half - max(first + count - 1, 1)
    both_flip = jnp.concatenate([flip[...]] * 2, axis=1)
    mirror = []
    for g in range(count):
        at = half - max(first + g, 1)
        pair = jnp.concatenate(split(across[at - lowest]), axis=0)
        turned = dot(both_flip, pair)
        lines = lax.broadcasted_iota(jnp.int32, turned.shape, 0) % width
        turned = jnp.where(lines == 0, edge[at], turned)
        mirror.append(turned if first + g > 0 else jnp.zeros_like(turned))
    plain = [own[first + g] for g in range(count) for _ in range(2)]
    plain = split(jnp.concatenate(plain, axis=0))
    mirror = split(jnp.concatenate(mirror, axis=0))
    left = jnp.concatenate([same[...]] * 2 + [back[...]] * 2, axis=1)
    values = dot(left, jnp.concatenate(plain + mirror, axis=1), 1)
    for g in range(count):
        keep = scale
        if first + g == half:
            keep = jnp.where(where_ref[2] == 1, scale, 0.0)
        out[g] = values[:, g * lanes : (g + 1) * lanes] * keep


def filter_kernel(lines, factor, th, tl, out):
    sects, extent, lanes = lines.shape
    count, mesh_size, _ = factor.shape
    width = mesh_size // sects
    past = count * width
    padded = (extent - past) // PAST
    empty = jnp.zeros((8 - PAST, lanes), jnp.float32)
    table = (th[...], tl[...])
    columns = []
    for g in range(count):
        pieces = []
        for s in range(sects):
            before = [past + i * padded + g for i in range(PAST)]
            before = [lines[(s - 1) % sects, at : at + 1, :] for at in before]
            at = g * width
            pieces.append(lines[s, at : at + 8, :] + jnp.concatenate(before + [empty], axis=0))
            pieces.append(lines[s, at + 8 : at + width, :])
        columns.append(jnp.concatenate(pieces, axis=0))
    both = dot3(table, split(jnp.concatenate(columns, axis=1)))
    half = lanes // 2
    sign = jnp.where(
        lax.broadcasted_iota(jnp.int32, (mesh_size, lanes), 1) < half, 1.0, -1.0
    )
    columns = []
    for g in range(count):
        cos = both[0:mesh_size, g * lanes : (g + 1) * lanes]
        sin = both[mesh_size:, g * lanes : (g + 1) * lanes]
        columns.append((cos + sign * pltpu.roll(sin, half, 1)) * factor[g])
    both = dot3(table, split(jnp.concatenate(columns, axis=1)))
    out[:, past:, :] = jnp.zeros((sects, extent - past, lanes), jnp.float32)
    for g in range(count):
        cos = both[0:mesh_size, g * lanes : (g + 1) * lanes]
        sin = both[mesh_size:, g * lanes : (g + 1) * lanes]
        field = cos - sign * pltpu.roll(sin, half, 1)
        for s in range(sects):
            after = ((s + 1) % sects) * width
            out[s, g * width : (g + 1) * width, :] = field[s * width : (s + 1) * width]
            for i in range(PAST):
                at = past + i * padded + g
                out[s, at : at + 1, :] = field[after + i : after + i + 1]


def gather_kernel(first, count, slots_padded, lines, bh, bl, wx, vx, zq, zv, bwh, bwl, bvh, bvl, *rest):
    *earlier, out, eh, el = rest
    sects, extent, lanes = lines.shape
    mesh_size = bwh.shape[0]
    width = mesh_size // sects
    past = count * width
    padded = (extent - past) // PAST

    @pl.when(pl.program_id(0) == 0)
    def _():
        joined = jnp.concatenate([lines[s] for s in range(sects)], axis=1)
        field = dot3(split(joined), (bh[...], bl[...]))
        pieces = []
        for g in range(count):
            for c in range(2):
                line = field[g * width : (g + 1) * width, c * mesh_size : (c + 1) * mesh_size]
                pieces.append(line)
        pieces += [field[past:, c * mesh_size : (c + 1) * mesh_size] for c in range(2)]
        high, low = split(jnp.concatenate(pieces, axis=0))
        eh[...] = high
        el[...] = low

    weights = (bwh[...], bwl[...])
    slopes = (bvh[...], bvl[...])
    steps = wx.shape[1]
    sums = [jnp.zeros((width, steps), jnp.float32) for _ in range(3)]
    strips = [[jnp.zeros((padded, steps), jnp.float32)] * PAST for _ in range(3)]
    for low, high in groups(count, GATHER_GROUP):
        part = slice(2 * low * width, 2 * (high * width if high < count else extent))
        left = (eh[part, :], el[part, :])
        along = dot3(left, weights)
        slope = dot3(left, slopes)
        for g in range(low, high):
            for c in range(2):
                at = c * slots_padded + first + g
                base = (2 * (g - low) + c) * width
                line = along[base : base + width]
                sums[0] = sums[0] + line * zq[at : at + 1, :]
                sums[1] = sums[1] + slope[base : base + width] * zq[at : at + 1, :]
                sums[2] = sums[2] + line * zv[at : at + 1, :]
        if high == count:
            for c in range(2):
                at = c * slots_padded + first
                for i in range(PAST):
                    base = 2 * (high - low) * width + (c * PAST + i) * padded
                    line = along[base : base + padded]
                    other = slope[base : base + padded]
                    strips[0][i] = strips[0][i] + line * zq[at : at + padded, :]
                    strips[1][i] = strips[1][i] + other * zq[at : at + padded, :]
                    strips[2][i] = strips[2][i] + line * zv[at : at + padded, :]
    forces = []
    for body, strip, shape in zip(sums, strips, (vx, wx, wx)):
        force = jnp.sum(body * shape[0:width, :], axis=0, keepdims=True)
        for i in range(PAST):
            at = width + i
            force = force + shape[at : at + 1, :] * jnp.sum(strip[i], axis=0, keepdims=True)
        forces.append(-force)
    result = jnp.concatenate(forces + [jnp.zeros_like(forces[0])], axis=0)
    width = out.shape[2]
    for d in range(out.shape[0]):
        part = result[:, d * width : (d + 1) * width]
        out[d] = part + earlier[0][d] if earlier else part


def cost(micros):
    return pl.CostEstimate(flops=int(micros * 1.0e9), transcendentals=0, bytes_accessed=int(micros * 1.0e5))


def params():
    return pltpu.CompilerParams(vmem_limit_bytes=VMEM)


def whole(array):
    return pl.BlockSpec(array.shape, lambda *_: (0,) * array.ndim)


def along_atoms(rows, step):
    return pl.BlockSpec((rows, step), lambda n: (0, n))


SMEM = pl.BlockSpec(memory_space=pltpu.SMEM)
IN_VMEM = pl.BlockSpec(memory_space=pltpu.VMEM)


def near_core(array):
    return pltpu.with_memory_space_constraint(array, pltpu.VMEM)


def pair_kernel(centre, others, mesh_size):
    half_mesh = float(mesh_size // 2)
    displace = []
    for component in range(3):
        offset = centre[component][None, :, None] - others[component][:, None, :]
        wrapped = jnp.mod(offset + half_mesh, float(mesh_size)) - half_mesh
        displace.append(
            wrapped + (centre[component + 3][None, :, None] - others[component + 3][:, None, :])
        )
    square = (
        displace[0] * displace[0]
        + displace[1] * displace[1]
        + displace[2] * displace[2]
        + soft_square
    )
    distance = jnp.sqrt(square)
    kernel = (
        lax.erfc(ewald_beta * distance) / (square * distance)
        + 2.0
        * ewald_beta
        / math.sqrt(math.pi)
        * jnp.exp(-ewald_beta * ewald_beta * square)
        / square
    )
    coupling = centre[6][None, :, None] * others[6][:, None, :] * kernel
    return jnp.stack([jnp.sum(coupling * shift_vector, axis=(0, 2)) for shift_vector in displace])


def shards(cells, fracs, charges, pair_blocks, influence):
    sects = lax.axis_size("sect")
    doms = lax.axis_size("dom")
    sect = lax.axis_index("sect")
    dom = lax.axis_index("dom")
    z_width, x_width, mesh_size = influence.shape
    atom_count = charges.shape[2]
    block_count = atom_count // BLOCK
    listed_count = pair_blocks.shape[3]
    half = z_width // 2
    slots = half + 1
    firsts = [-(-slots * n // CHUNKS) for n in range(CHUNKS + 1)]
    counts = [b - a for a, b in zip(firsts, firsts[1:])]
    padded = [-(-count // 8) * 8 for count in counts]
    slots_padded = -(-max(a + b for a, b in zip(firsts, padded)) // 8) * 8
    lanes = 2 * x_width
    total = doms * atom_count
    where_am_i = jnp.stack([sect, dom, (dom >= doms // 2).astype(jnp.int32)])

    f32, bf16 = jnp.float32, jnp.bfloat16
    copies = pl.pallas_call(
        pack_kernel,
        out_shape=jax.ShapeDtypeStruct((doms, block_count, 8, BLOCK), f32),
        name="pack",
    )(cells, fracs, charges)
    row = lax.all_to_all(copies, "dom", 0, 0, tiled=True)
    packed = copies[0]

    edges = []
    for s in range(sects):
        for d in range(doms):
            edges.append((s * doms + d, ((sects - s) % sects) * doms + doms - 1 - d))
    flip = np.zeros((2 * x_width, x_width), np.float32)
    for i in range(1, x_width):
        flip[i, x_width - i] = 1.0
        flip[x_width + i, x_width - i] = 1.0
    same = np.eye(mesh_size, dtype=np.float32)
    back = np.roll(same[::-1], 1, axis=0)
    flip, same, back = (jnp.asarray(m).astype(jnp.bfloat16) for m in (flip, same, back))
    planes = []
    for first, count in zip(firsts, counts):
        lowest = half - max(first + count - 1, 1)
        highest = half - max(first, 1)
        planes.append(influence[half + lowest : half + highest + 1])
    sect_flip = [(s, sects - 1 - s) for s in range(sects)]
    dom_flip = [(d, doms - 1 - d) for d in range(doms)]
    planes = [lax.ppermute(p, "sect", sect_flip) for p in planes]

    step = np.arange(mesh_size)
    angle = 2.0 * np.pi * (np.outer(step, step) % mesh_size) / mesh_size
    cos, sin = np.cos(angle), np.sin(angle)

    def by_sect(real, imag):
        real = real.reshape(mesh_size, sects, 1, x_width)
        imag = imag.reshape(mesh_size, sects, 1, x_width)
        return np.concatenate([real, imag], axis=2).reshape(mesh_size, 2 * mesh_size)

    rh, rl = split_table(by_sect(cos, -sin))
    ih, il = split_table(by_sect(sin, cos))
    bh, bl = split_table(np.concatenate([by_sect(cos, -sin).T, by_sect(sin, cos).T], axis=1))
    th, tl = split_table(np.concatenate([cos, sin], axis=0))

    atom_step = 512
    grid = (total // atom_step,)
    shapes = [
        ((x_width + 8, total), f32),
        ((2 * slots_padded, total), f32),
        ((mesh_size, total), bf16),
        ((mesh_size, total), bf16),
    ]

    def basis(which, blocks):
        return pl.pallas_call(
            lambda *refs: basis_kernel(which, mesh_size, x_width, z_width, slots_padded, *refs),
            grid=grid,
            in_specs=[
                SMEM,
                pl.BlockSpec(
                    (atom_step // atom_count, block_count, 8, BLOCK), lambda n: (n, 0, 0, 0)
                ),
            ],
            out_specs=[along_atoms(shape[0], atom_step) for shape, _ in shapes],
            out_shape=[jax.ShapeDtypeStruct(shape, dtype) for shape, dtype in shapes],
            compiler_params=params(),
            cost_estimate=cost(0.1 if which else 4),
            name="basis",
        )(where_am_i, blocks)

    wx, zq, bwh, bwl = basis(0, row)

    sent = []
    for first, count in zip(firsts, counts):
        extent = count * x_width + PAST * (-(-count // 8) * 8)
        shape = (sects, extent, lanes)
        lines = pl.pallas_call(
            lambda *refs, first=first, count=count: spread_kernel(first, count, slots_padded, *refs),
            grid=grid,
            in_specs=[
                along_atoms(x_width + 8, atom_step),
                along_atoms(2 * slots_padded, atom_step),
                along_atoms(mesh_size, atom_step),
                along_atoms(mesh_size, atom_step),
            ]
            + [whole(t) for t in (rh, rl, ih, il)],
            out_specs=pl.BlockSpec(shape, lambda n: (0, 0, 0)),
            out_shape=jax.ShapeDtypeStruct(shape, f32),
            scratch_shapes=[pltpu.VMEM((extent, mesh_size), f32)] * 2,
            compiler_params=params(),
            cost_estimate=cost(9),
            name="spread",
        )(wx, zq, bwh, bwl, rh, rl, ih, il)
        sent.append(lines)
    corner, beside, planes[0], sent[0] = lax.optimization_barrier(
        (influence[half:, 0:1], row, planes[0], sent[0])
    )
    vx, zv, bvh, bvl = basis(1, beside)
    vx, sent[-1] = lax.optimization_barrier((vx, sent[-1]))
    planes[0] = lax.ppermute(planes[0], "dom", dom_flip)
    edge = lax.ppermute(corner, ("sect", "dom"), edges)
    sent = [lax.all_to_all(lines, "sect", split_axis=0, concat_axis=0, tiled=True) for lines in sent]
    planes[1:], beside, sent[0] = lax.optimization_barrier((planes[1:], beside, sent[0]))
    planes[1:] = [lax.ppermute(p, "dom", dom_flip) for p in planes[1:]]
    planes[0], edge, sent[0] = lax.optimization_barrier((planes[0], edge, sent[0]))
    ahead = [(s, (s + 1) % sects) for s in range(sects)]
    behind = [(b, a) for a, b in ahead]
    near = [lax.ppermute(beside, "sect", ahead), lax.ppermute(beside, "sect", behind)]

    def folded(first, count, mirror):
        return pl.pallas_call(
            lambda *refs: influence_kernel(first, half, float(mesh_size) ** -3, *refs),
            in_specs=[SMEM] + [pl.BlockSpec(memory_space=pltpu.VMEM)] * 6,
            out_specs=pl.BlockSpec(memory_space=pltpu.VMEM),
            out_shape=jax.ShapeDtypeStruct((count, mesh_size, lanes), f32),
            compiler_params=params(),
            cost_estimate=cost(3.5),
            name="influence",
        )(where_am_i, influence, mirror, near_core(edge), flip, same, back)

    factors = [folded(firsts[0], counts[0], planes[0])]
    for n in range(1, CHUNKS):
        factors.append(folded(firsts[n], counts[n], planes[n]))
    fields = []
    near, row, packed, sent[-1] = lax.optimization_barrier((near, row, packed, sent[-1]))
    for lines, factor in zip(sent, factors):
        field = pl.pallas_call(
            filter_kernel,
            grid=(1,),
            in_specs=[
                IN_VMEM,
                IN_VMEM,
                whole(th),
                whole(tl),
            ],
            out_specs=whole(lines),
            out_shape=jax.ShapeDtypeStruct(lines.shape, f32),
            compiler_params=params(),
            cost_estimate=cost(5.5),
            name="filter",
        )(near_core(lines), factor, th, tl)
        fields.append(field)
    fields = [lax.all_to_all(field, "sect", split_axis=0, concat_axis=0, tiled=True) for field in fields]

    listed = pair_blocks[0, 0]
    neighbour = listed // block_count
    near = jnp.stack([near[0], row, near[1]])
    from_dom = (dom + neighbour % 3 - 1) % doms
    source = (neighbour // 3 * doms + from_dom) * block_count + listed % block_count
    pool = near.reshape(3 * doms * block_count, 8 * BLOCK)
    pick = (source.reshape(-1, 1) == jnp.arange(pool.shape[0], dtype=jnp.int32)[None]).astype(f32)
    chosen = lax.dot_general(
        pick, pool, (((1,), (0,)), ((), ())), precision=lax.Precision.HIGHEST, preferred_element_type=f32
    ).reshape(block_count, listed_count, 8, BLOCK)
    chosen = jnp.transpose(chosen, (0, 2, 1, 3))
    block_forces = jnp.stack(
        [pair_kernel(packed[b], chosen[b], mesh_size) for b in range(block_count)], axis=1
    )
    short_force = block_forces.reshape(3, atom_count)

    earlier = []
    by_dom = pl.BlockSpec((atom_step // atom_count, 4, atom_count), lambda n: (n, 0, 0))
    for lines, first, count in zip(fields, firsts, counts):
        earlier = [pl.pallas_call(
            lambda *refs, first=first, count=count: gather_kernel(first, count, slots_padded, *refs),
            grid=grid,
            in_specs=[IN_VMEM, whole(bh), whole(bl)]
            + [along_atoms(a.shape[0], atom_step) for a in (wx, vx, zq, zv, bwh, bwl, bvh, bvl)]
            + [by_dom] * len(earlier),
            out_specs=by_dom,
            out_shape=jax.ShapeDtypeStruct((doms, 4, atom_count), f32),
            scratch_shapes=[pltpu.VMEM((2 * lines.shape[1], mesh_size), bf16)] * 2,
            compiler_params=params(),
            cost_estimate=cost(13),
            name="gather",
        )(near_core(lines), bh, bl, wx, vx, zq, zv, bwh, bwl, bvh, bvl, *earlier)]
    shares = lax.all_to_all(earlier[0], "dom", 0, 0, tiled=True)
    mesh_force = jnp.sum(shares, axis=0)[:3]
    return (short_force + mesh_force).reshape(3, 1, 1, atom_count)


def solution(mesh):
    in_specs = (
        P(None, "sect", "dom", None),
        P(None, "sect", "dom", None),
        P("sect", "dom", None),
        P("sect", "dom", None, None),
        P("dom", "sect", None),
    )
    out_specs = P(None, "sect", "dom", None)
    return jax.shard_map(shards, mesh=mesh, in_specs=in_specs, out_specs=out_specs, check_vma=False)
```

```python
import math

import jax
import jax.numpy as jnp
import numpy as np
from jax import lax
from jax.experimental import pallas as pl
from jax.experimental.pallas import tpu as pltpu
from jax.sharding import PartitionSpec as P

BLOCK = 128
PAST = 3
CHUNKS = 2
VMEM = 56 * 1024 * 1024
SPREAD_GROUP = 5
GATHER_GROUP = 5

ewald_beta = 0.1
soft_square = 9.0


def split_table(table):
    table = jnp.asarray(np.asarray(table, np.float32))
    high = table.astype(jnp.bfloat16)
    low = (table - high.astype(jnp.float32)).astype(jnp.bfloat16)
    return high, low


def split(value):
    high = value.astype(jnp.bfloat16)
    low = (value - high.astype(jnp.float32)).astype(jnp.bfloat16)
    return high, low


def dot(left, right, right_dim=0):
    return lax.dot_general(
        left, right, (((1,), (right_dim,)), ((), ())), preferred_element_type=jnp.float32
    )


def dot3(left, right, right_dim=0):
    left = jnp.concatenate([left[0], left[0], left[1]], axis=1)
    right = jnp.concatenate([right[0], right[1], right[0]], axis=right_dim)
    return dot(left, right, right_dim)


def spline(frac):
    inner = 1.0 - frac
    square = frac * frac
    cube = square * frac
    weights = (
        inner * inner * inner / 6.0,
        (3.0 * cube - 6.0 * square + 4.0) / 6.0,
        (-3.0 * cube + 3.0 * square + 3.0 * frac + 1.0) / 6.0,
        cube / 6.0,
    )
    slopes = (
        -inner * inner / 2.0,
        (3.0 * square - 4.0 * frac) / 2.0,
        (-3.0 * square + 2.0 * frac + 1.0) / 2.0,
        square / 2.0,
    )
    return weights, slopes


def turn(steps, mesh_size):
    part = steps * (1.0 / mesh_size)
    part = part - jnp.floor(part)
    half = math.pi * jnp.where(part > 0.5, part - 1.0, part)
    sq = half * half
    sin = half
    cos = jnp.ones_like(half)
    term = half
    for n in range(1, 7):
        term = term * sq * (-1.0 / ((2 * n) * (2 * n + 1)))
        sin = sin + term
    term = cos
    for n in range(1, 8):
        term = term * sq * (-1.0 / ((2 * n - 1) * (2 * n)))
        cos = cos + term
    return 1.0 - 2.0 * sin * sin, 2.0 * sin * cos


def place(offset, values):
    out = jnp.zeros(offset.shape, jnp.float32)
    for k in range(4):
        out = jnp.where(offset == k, values[k], out)
    return out


def pack_kernel(cells, fracs, charges, out):
    rows = [cells[n, 0].astype(jnp.float32) for n in range(3)] + [fracs[n, 0] for n in range(3)]
    atoms = jnp.concatenate(rows + [charges[0], jnp.zeros_like(charges[0])], axis=0)
    for b in range(out.shape[1]):
        part = atoms[:, b * BLOCK : (b + 1) * BLOCK]
        for d in range(out.shape[0]):
            out[d, b] = part


def basis_kernel(which, mesh_size, x_width, z_width, slots_padded, where_ref, blocks, along_x, along_z, high_y, low_y):
    atoms = jnp.concatenate(
        [blocks[d, b] for d in range(blocks.shape[0]) for b in range(blocks.shape[1])], axis=1
    )

    def row(n):
        return atoms[n : n + 1, :]

    lanes = atoms.shape[1]
    charge = row(6)

    def rows(count):
        return lax.broadcasted_iota(jnp.int32, (count, lanes), 0).astype(jnp.float32)

    values = spline(row(3))[which]
    offset = rows(along_x.shape[0]) - (row(0) - (where_ref[0] * x_width).astype(jnp.float32))
    along_x[...] = place(offset, values)
    values = spline(row(4))[which]
    offset = lax.broadcasted_iota(jnp.int32, (mesh_size, lanes), 0) - row(1).astype(jnp.int32)
    high, low = split(place(offset & (mesh_size - 1), values))
    high_y[...] = high
    low_y[...] = low
    values = spline(row(5))[which]
    wave = rows(slots_padded) + (where_ref[1] * z_width).astype(jnp.float32)
    real = jnp.zeros_like(wave)
    imag = jnp.zeros_like(wave)
    cos, sin = turn(wave * row(2), mesh_size)
    by_cos, by_sin = turn(wave[:, 0:128], mesh_size)
    by_cos = jnp.concatenate([by_cos] * (lanes // 128), axis=1)
    by_sin = jnp.concatenate([by_sin] * (lanes // 128), axis=1)
    for k in range(4):
        if k:
            cos, sin = cos * by_cos - sin * by_sin, sin * by_cos + cos * by_sin
        real = real + (charge * values[k]) * cos
        imag = imag - (charge * values[k]) * sin
    along_z[0:slots_padded, :] = real
    along_z[slots_padded:, :] = imag


def groups(count, size):
    return [(low, min(low + size, count)) for low in range(0, count, size)]


def spread_kernel(first, count, slots_padded, wx, zq, bwh, bwl, rh, rl, ih, il, out, *sums):
    step = pl.program_id(0)
    padded = -(-count // 8) * 8
    width = sums[0].shape[0] - PAST * padded
    width = width // count
    wide = wx[0:width, :]
    right = (bwh[...], bwl[...])

    @pl.when(step == 0)
    def _():
        for acc in sums:
            acc[...] = jnp.zeros_like(acc)

    for low, high in groups(count, SPREAD_GROUP):
        pieces = []
        for c in range(2):
            base = c * slots_padded + first
            pieces += [wide * zq[base + g : base + g + 1, :] for g in range(low, high)]
            if high == count:
                strip = zq[base : base + padded, :]
                pieces += [wx[width + i : width + i + 1, :] * strip for i in range(PAST)]
        part = dot3(split(jnp.concatenate(pieces, axis=0)), right, 1)
        rows = part.shape[0] // 2
        for c in range(2):
            sums[c][low * width : low * width + rows, :] += part[c * rows : (c + 1) * rows]

    @pl.when(step == pl.num_programs(0) - 1)
    def _():
        real, imag = (split(acc[...]) for acc in sums)
        lines = dot3(real, (rh[...], rl[...])) + dot3(imag, (ih[...], il[...]))
        lanes = out.shape[2]
        for s in range(out.shape[0]):
            out[s] = lines[:, s * lanes : (s + 1) * lanes]


def influence_kernel(first, half, scale, where_ref, own, across, edge, flip, same, back, out):
    count, _, lanes = out.shape
    width = own.shape[1]
    lowest = half - max(first + count - 1, 1)
    both_flip = jnp.concatenate([flip[...]] * 2, axis=1)
    mirror = []
    for g in range(count):
        at = half - max(first + g, 1)
        pair = jnp.concatenate(split(across[at - lowest]), axis=0)
        turned = dot(both_flip, pair)
        lines = lax.broadcasted_iota(jnp.int32, turned.shape, 0) % width
        turned = jnp.where(lines == 0, edge[at], turned)
        mirror.append(turned if first + g > 0 else jnp.zeros_like(turned))
    plain = [own[first + g] for g in range(count) for _ in range(2)]
    plain = split(jnp.concatenate(plain, axis=0))
    mirror = split(jnp.concatenate(mirror, axis=0))
    left = jnp.concatenate([same[...]] * 2 + [back[...]] * 2, axis=1)
    values = dot(left, jnp.concatenate(plain + mirror, axis=1), 1)
    for g in range(count):
        keep = scale
        if first + g == half:
            keep = jnp.where(where_ref[2] == 1, scale, 0.0)
        out[g] = values[:, g * lanes : (g + 1) * lanes] * keep


def filter_kernel(lines, factor, th, tl, out):
    sects, extent, lanes = lines.shape
    count, mesh_size, _ = factor.shape
    width = mesh_size // sects
    past = count * width
    padded = (extent - past) // PAST
    empty = jnp.zeros((8 - PAST, lanes), jnp.float32)
    table = (th[...], tl[...])
    columns = []
    for g in range(count):
        pieces = []
        for s in range(sects):
            before = [past + i * padded + g for i in range(PAST)]
            before = [lines[(s - 1) % sects, at : at + 1, :] for at in before]
            at = g * width
            pieces.append(lines[s, at : at + 8, :] + jnp.concatenate(before + [empty], axis=0))
            pieces.append(lines[s, at + 8 : at + width, :])
        columns.append(jnp.concatenate(pieces, axis=0))
    both = dot3(table, split(jnp.concatenate(columns, axis=1)))
    half = lanes // 2
    sign = jnp.where(
        lax.broadcasted_iota(jnp.int32, (mesh_size, lanes), 1) < half, 1.0, -1.0
    )
    columns = []
    for g in range(count):
        cos = both[0:mesh_size, g * lanes : (g + 1) * lanes]
        sin = both[mesh_size:, g * lanes : (g + 1) * lanes]
        columns.append((cos + sign * pltpu.roll(sin, half, 1)) * factor[g])
    both = dot3(table, split(jnp.concatenate(columns, axis=1)))
    out[:, past:, :] = jnp.zeros((sects, extent - past, lanes), jnp.float32)
    for g in range(count):
        cos = both[0:mesh_size, g * lanes : (g + 1) * lanes]
        sin = both[mesh_size:, g * lanes : (g + 1) * lanes]
        field = cos - sign * pltpu.roll(sin, half, 1)
        for s in range(sects):
            after = ((s + 1) % sects) * width
            out[s, g * width : (g + 1) * width, :] = field[s * width : (s + 1) * width]
            for i in range(PAST):
                at = past + i * padded + g
                out[s, at : at + 1, :] = field[after + i : after + i + 1]


def gather_kernel(first, count, slots_padded, lines, bh, bl, wx, vx, zq, zv, bwh, bwl, bvh, bvl, *rest):
    *earlier, out, eh, el = rest
    sects, extent, lanes = lines.shape
    mesh_size = bwh.shape[0]
    width = mesh_size // sects
    past = count * width
    padded = (extent - past) // PAST

    @pl.when(pl.program_id(0) == 0)
    def _():
        joined = jnp.concatenate([lines[s] for s in range(sects)], axis=1)
        field = dot3(split(joined), (bh[...], bl[...]))
        pieces = []
        for g in range(count):
            for c in range(2):
                line = field[g * width : (g + 1) * width, c * mesh_size : (c + 1) * mesh_size]
                pieces.append(line)
        pieces += [field[past:, c * mesh_size : (c + 1) * mesh_size] for c in range(2)]
        high, low = split(jnp.concatenate(pieces, axis=0))
        eh[...] = high
        el[...] = low

    weights = (bwh[...], bwl[...])
    slopes = (bvh[...], bvl[...])
    steps = wx.shape[1]
    sums = [jnp.zeros((width, steps), jnp.float32) for _ in range(3)]
    strips = [[jnp.zeros((padded, steps), jnp.float32)] * PAST for _ in range(3)]
    for low, high in groups(count, GATHER_GROUP):
        part = slice(2 * low * width, 2 * (high * width if high < count else extent))
        left = (eh[part, :], el[part, :])
        along = dot3(left, weights)
        slope = dot3(left, slopes)
        for g in range(low, high):
            for c in range(2):
                at = c * slots_padded + first + g
                base = (2 * (g - low) + c) * width
                line = along[base : base + width]
                sums[0] = sums[0] + line * zq[at : at + 1, :]
                sums[1] = sums[1] + slope[base : base + width] * zq[at : at + 1, :]
                sums[2] = sums[2] + line * zv[at : at + 1, :]
        if high == count:
            for c in range(2):
                at = c * slots_padded + first
                for i in range(PAST):
                    base = 2 * (high - low) * width + (c * PAST + i) * padded
                    line = along[base : base + padded]
                    other = slope[base : base + padded]
                    strips[0][i] = strips[0][i] + line * zq[at : at + padded, :]
                    strips[1][i] = strips[1][i] + other * zq[at : at + padded, :]
                    strips[2][i] = strips[2][i] + line * zv[at : at + padded, :]
    forces = []
    for body, strip, shape in zip(sums, strips, (vx, wx, wx)):
        force = jnp.sum(body * shape[0:width, :], axis=0, keepdims=True)
        for i in range(PAST):
            at = width + i
            force = force + shape[at : at + 1, :] * jnp.sum(strip[i], axis=0, keepdims=True)
        forces.append(-force)
    result = jnp.concatenate(forces + [jnp.zeros_like(forces[0])], axis=0)
    width = out.shape[2]
    for d in range(out.shape[0]):
        part = result[:, d * width : (d + 1) * width]
        out[d] = part + earlier[0][d] if earlier else part


def cost(micros):
    return pl.CostEstimate(flops=int(micros * 1.0e9), transcendentals=0, bytes_accessed=int(micros * 1.0e5))


def params():
    return pltpu.CompilerParams(vmem_limit_bytes=VMEM)


def whole(array):
    return pl.BlockSpec(array.shape, lambda *_: (0,) * array.ndim)


def along_atoms(rows, step):
    return pl.BlockSpec((rows, step), lambda n: (0, n))


SMEM = pl.BlockSpec(memory_space=pltpu.SMEM)
IN_VMEM = pl.BlockSpec(memory_space=pltpu.VMEM)


def near_core(array):
    return pltpu.with_memory_space_constraint(array, pltpu.VMEM)


def pair_kernel(centre, others, mesh_size):
    half_mesh = float(mesh_size // 2)
    displace = []
    for component in range(3):
        offset = centre[component][None, :, None] - others[component][:, None, :]
        wrapped = jnp.mod(offset + half_mesh, float(mesh_size)) - half_mesh
        displace.append(
            wrapped + (centre[component + 3][None, :, None] - others[component + 3][:, None, :])
        )
    square = (
        displace[0] * displace[0]
        + displace[1] * displace[1]
        + displace[2] * displace[2]
        + soft_square
    )
    distance = jnp.sqrt(square)
    kernel = (
        lax.erfc(ewald_beta * distance) / (square * distance)
        + 2.0
        * ewald_beta
        / math.sqrt(math.pi)
        * jnp.exp(-ewald_beta * ewald_beta * square)
        / square
    )
    coupling = centre[6][None, :, None] * others[6][:, None, :] * kernel
    return jnp.stack([jnp.sum(coupling * shift_vector, axis=(0, 2)) for shift_vector in displace])


def shards(cells, fracs, charges, pair_blocks, influence):
    sects = lax.axis_size("sect")
    doms = lax.axis_size("dom")
    sect = lax.axis_index("sect")
    dom = lax.axis_index("dom")
    z_width, x_width, mesh_size = influence.shape
    atom_count = charges.shape[2]
    block_count = atom_count // BLOCK
    listed_count = pair_blocks.shape[3]
    half = z_width // 2
    slots = half + 1
    firsts = [-(-slots * n // CHUNKS) for n in range(CHUNKS + 1)]
    counts = [b - a for a, b in zip(firsts, firsts[1:])]
    padded = [-(-count // 8) * 8 for count in counts]
    slots_padded = -(-max(a + b for a, b in zip(firsts, padded)) // 8) * 8
    lanes = 2 * x_width
    total = doms * atom_count
    where_am_i = jnp.stack([sect, dom, (dom >= doms // 2).astype(jnp.int32)])

    f32, bf16 = jnp.float32, jnp.bfloat16
    copies = pl.pallas_call(
        pack_kernel,
        out_shape=jax.ShapeDtypeStruct((doms, block_count, 8, BLOCK), f32),
        name="pack",
    )(cells, fracs, charges)
    row = lax.all_to_all(copies, "dom", 0, 0, tiled=True)

    edges = []
    for s in range(sects):
        for d in range(doms):
            edges.append((s * doms + d, ((sects - s) % sects) * doms + doms - 1 - d))
    flip = np.zeros((2 * x_width, x_width), np.float32)
    for i in range(1, x_width):
        flip[i, x_width - i] = 1.0
        flip[x_width + i, x_width - i] = 1.0
    same = np.eye(mesh_size, dtype=np.float32)
    back = np.roll(same[::-1], 1, axis=0)
    flip, same, back = (jnp.asarray(m).astype(jnp.bfloat16) for m in (flip, same, back))
    planes = []
    for first, count in zip(firsts, counts):
        lowest = half - max(first + count - 1, 1)
        highest = half - max(first, 1)
        planes.append(influence[half + lowest : half + highest + 1])
    sect_flip = [(s, sects - 1 - s) for s in range(sects)]
    dom_flip = [(d, doms - 1 - d) for d in range(doms)]
    planes = [lax.ppermute(p, "sect", sect_flip) for p in planes]

    step = np.arange(mesh_size)
    angle = 2.0 * np.pi * (np.outer(step, step) % mesh_size) / mesh_size
    cos, sin = np.cos(angle), np.sin(angle)

    def by_sect(real, imag):
        real = real.reshape(mesh_size, sects, 1, x_width)
        imag = imag.reshape(mesh_size, sects, 1, x_width)
        return np.concatenate([real, imag], axis=2).reshape(mesh_size, 2 * mesh_size)

    rh, rl = split_table(by_sect(cos, -sin))
    ih, il = split_table(by_sect(sin, cos))
    bh, bl = split_table(np.concatenate([by_sect(cos, -sin).T, by_sect(sin, cos).T], axis=1))
    th, tl = split_table(np.concatenate([cos, sin], axis=0))

    atom_step = 1024
    grid = (total // atom_step,)
    shapes = [
        ((x_width + 8, total), f32),
        ((2 * slots_padded, total), f32),
        ((mesh_size, total), bf16),
        ((mesh_size, total), bf16),
    ]

    def basis(which, blocks):
        return pl.pallas_call(
            lambda *refs: basis_kernel(which, mesh_size, x_width, z_width, slots_padded, *refs),
            grid=grid,
            in_specs=[
                SMEM,
                pl.BlockSpec(
                    (atom_step // atom_count, block_count, 8, BLOCK), lambda n: (n, 0, 0, 0)
                ),
            ],
            out_specs=[along_atoms(shape[0], atom_step) for shape, _ in shapes],
            out_shape=[jax.ShapeDtypeStruct(shape, dtype) for shape, dtype in shapes],
            compiler_params=params(),
            cost_estimate=cost(0.1 if which else 4),
            name="basis",
        )(where_am_i, blocks)

    wx, zq, bwh, bwl = basis(0, row)

    sent = []
    for first, count in zip(firsts, counts):
        extent = count * x_width + PAST * (-(-count // 8) * 8)
        shape = (sects, extent, lanes)
        lines = pl.pallas_call(
            lambda *refs, first=first, count=count: spread_kernel(first, count, slots_padded, *refs),
            grid=grid,
            in_specs=[
                along_atoms(x_width + 8, atom_step),
                along_atoms(2 * slots_padded, atom_step),
                along_atoms(mesh_size, atom_step),
                along_atoms(mesh_size, atom_step),
            ]
            + [whole(t) for t in (rh, rl, ih, il)],
            out_specs=pl.BlockSpec(shape, lambda n: (0, 0, 0)),
            out_shape=jax.ShapeDtypeStruct(shape, f32),
            scratch_shapes=[pltpu.VMEM((extent, mesh_size), f32)] * 2,
            compiler_params=params(),
            cost_estimate=cost(9),
            name="spread",
        )(wx, zq, bwh, bwl, rh, rl, ih, il)
        sent.append(lines)
    later, beside, planes[0], sent[0] = lax.optimization_barrier(
        (influence, row, planes[0], sent[0])
    )
    corner = later[half:, 0:1]
    vx, zv, bvh, bvl = basis(1, beside)
    vx, sent[-1] = lax.optimization_barrier((vx, sent[-1]))
    planes[0] = lax.ppermute(planes[0], "dom", dom_flip)
    edge = lax.ppermute(corner, ("sect", "dom"), edges)
    sent = [lax.all_to_all(lines, "sect", split_axis=0, concat_axis=0, tiled=True) for lines in sent]
    planes[1:], beside, sent[0] = lax.optimization_barrier((planes[1:], beside, sent[0]))
    planes[1:] = [lax.ppermute(p, "dom", dom_flip) for p in planes[1:]]
    planes[0], edge, sent[0] = lax.optimization_barrier((planes[0], edge, sent[0]))
    ahead = [(s, (s + 1) % sects) for s in range(sects)]
    behind = [(b, a) for a, b in ahead]
    near = [lax.ppermute(beside, "sect", ahead), lax.ppermute(beside, "sect", behind)]

    def folded(first, count, mirror):
        return pl.pallas_call(
            lambda *refs: influence_kernel(first, half, float(mesh_size) ** -3, *refs),
            in_specs=[SMEM] + [pl.BlockSpec(memory_space=pltpu.VMEM)] * 6,
            out_specs=pl.BlockSpec(memory_space=pltpu.VMEM),
            out_shape=jax.ShapeDtypeStruct((count, mesh_size, lanes), f32),
            compiler_params=params(),
            cost_estimate=cost(3.5),
            name="influence",
        )(where_am_i, influence, mirror, near_core(edge), flip, same, back)

    factors = [folded(firsts[0], counts[0], planes[0])]
    for n in range(1, CHUNKS):
        factors.append(folded(firsts[n], counts[n], planes[n]))
    fields = []
    near, row, copies, sent[-1] = lax.optimization_barrier((near, row, copies, sent[-1]))
    packed = copies[0]
    for lines, factor in zip(sent, factors):
        field = pl.pallas_call(
            filter_kernel,
            grid=(1,),
            in_specs=[
                IN_VMEM,
                IN_VMEM,
                whole(th),
                whole(tl),
            ],
            out_specs=whole(lines),
            out_shape=jax.ShapeDtypeStruct(lines.shape, f32),
            compiler_params=params(),
            cost_estimate=cost(5.5),
            name="filter",
        )(near_core(lines), factor, th, tl)
        fields.append(field)
    fields = [lax.all_to_all(field, "sect", split_axis=0, concat_axis=0, tiled=True) for field in fields]

    listed = pair_blocks[0, 0]
    neighbour = listed // block_count
    near = jnp.stack([near[0], row, near[1]])
    from_dom = (dom + neighbour % 3 - 1) % doms
    source = (neighbour // 3 * doms + from_dom) * block_count + listed % block_count
    pool = near.reshape(3 * doms * block_count, 8 * BLOCK)
    pick = (source.reshape(-1, 1) == jnp.arange(pool.shape[0], dtype=jnp.int32)[None]).astype(f32)
    chosen = lax.dot_general(
        pick, pool, (((1,), (0,)), ((), ())), precision=lax.Precision.HIGHEST, preferred_element_type=f32
    ).reshape(block_count, listed_count, 8, BLOCK)
    chosen = jnp.transpose(chosen, (0, 2, 1, 3))
    block_forces = jnp.stack(
        [pair_kernel(packed[b], chosen[b], mesh_size) for b in range(block_count)], axis=1
    )
    short_force = block_forces.reshape(3, atom_count)

    earlier = []
    by_dom = pl.BlockSpec((atom_step // atom_count, 4, atom_count), lambda n: (n, 0, 0))
    for lines, first, count in zip(fields, firsts, counts):
        earlier = [pl.pallas_call(
            lambda *refs, first=first, count=count: gather_kernel(first, count, slots_padded, *refs),
            grid=grid,
            in_specs=[IN_VMEM, whole(bh), whole(bl)]
            + [along_atoms(a.shape[0], atom_step) for a in (wx, vx, zq, zv, bwh, bwl, bvh, bvl)]
            + [by_dom] * len(earlier),
            out_specs=by_dom,
            out_shape=jax.ShapeDtypeStruct((doms, 4, atom_count), f32),
            scratch_shapes=[pltpu.VMEM((2 * lines.shape[1], mesh_size), bf16)] * 2,
            compiler_params=params(),
            cost_estimate=cost(13),
            name="gather",
        )(near_core(lines), bh, bl, wx, vx, zq, zv, bwh, bwl, bvh, bvl, *earlier)]
    shares = lax.all_to_all(earlier[0], "dom", 0, 0, tiled=True)
    mesh_force = jnp.sum(shares, axis=0)[:3]
    return (short_force + mesh_force).reshape(3, 1, 1, atom_count)


def solution(mesh):
    in_specs = (
        P(None, "sect", "dom", None),
        P(None, "sect", "dom", None),
        P("sect", "dom", None),
        P("sect", "dom", None, None),
        P("dom", "sect", None),
    )
    out_specs = P(None, "sect", "dom", None)
    return jax.shard_map(shards, mesh=mesh, in_specs=in_specs, out_specs=out_specs, check_vma=False)
```

```python
import math

import jax
import jax.numpy as jnp
import numpy as np
from jax import lax
from jax.experimental import pallas as pl
from jax.experimental.pallas import tpu as pltpu
from jax.sharding import PartitionSpec as P

BLOCK = 128
PAST = 3
CHUNKS = 2
VMEM = 56 * 1024 * 1024
SPREAD_GROUP = 5
GATHER_GROUP = 5

ewald_beta = 0.1
soft_square = 9.0


def split_table(table):
    table = jnp.asarray(np.asarray(table, np.float32))
    high = table.astype(jnp.bfloat16)
    low = (table - high.astype(jnp.float32)).astype(jnp.bfloat16)
    return high, low


def split(value):
    high = value.astype(jnp.bfloat16)
    low = (value - high.astype(jnp.float32)).astype(jnp.bfloat16)
    return high, low


def dot(left, right, right_dim=0):
    return lax.dot_general(
        left, right, (((1,), (right_dim,)), ((), ())), preferred_element_type=jnp.float32
    )


def dot3(left, right, right_dim=0):
    left = jnp.concatenate([left[0], left[0], left[1]], axis=1)
    right = jnp.concatenate([right[0], right[1], right[0]], axis=right_dim)
    return dot(left, right, right_dim)


def spline(frac):
    inner = 1.0 - frac
    square = frac * frac
    cube = square * frac
    weights = (
        inner * inner * inner / 6.0,
        (3.0 * cube - 6.0 * square + 4.0) / 6.0,
        (-3.0 * cube + 3.0 * square + 3.0 * frac + 1.0) / 6.0,
        cube / 6.0,
    )
    slopes = (
        -inner * inner / 2.0,
        (3.0 * square - 4.0 * frac) / 2.0,
        (-3.0 * square + 2.0 * frac + 1.0) / 2.0,
        square / 2.0,
    )
    return weights, slopes


def turn(steps, mesh_size):
    part = steps * (1.0 / mesh_size)
    part = part - jnp.floor(part)
    half = math.pi * jnp.where(part > 0.5, part - 1.0, part)
    sq = half * half
    sin = half
    cos = jnp.ones_like(half)
    term = half
    for n in range(1, 7):
        term = term * sq * (-1.0 / ((2 * n) * (2 * n + 1)))
        sin = sin + term
    term = cos
    for n in range(1, 8):
        term = term * sq * (-1.0 / ((2 * n - 1) * (2 * n)))
        cos = cos + term
    return 1.0 - 2.0 * sin * sin, 2.0 * sin * cos


def place(offset, values):
    out = jnp.zeros(offset.shape, jnp.float32)
    for k in range(4):
        out = jnp.where(offset == k, values[k], out)
    return out


def pack_kernel(cells, fracs, charges, out):
    rows = [cells[n, 0].astype(jnp.float32) for n in range(3)] + [fracs[n, 0] for n in range(3)]
    atoms = jnp.concatenate(rows + [charges[0], jnp.zeros_like(charges[0])], axis=0)
    for b in range(out.shape[1]):
        part = atoms[:, b * BLOCK : (b + 1) * BLOCK]
        for d in range(out.shape[0]):
            out[d, b] = part


def basis_kernel(which, mesh_size, x_width, z_width, slots_padded, where_ref, blocks, along_x, along_z, high_y, low_y):
    atoms = jnp.concatenate(
        [blocks[d, b] for d in range(blocks.shape[0]) for b in range(blocks.shape[1])], axis=1
    )

    def row(n):
        return atoms[n : n + 1, :]

    lanes = atoms.shape[1]
    charge = row(6)

    def rows(count):
        return lax.broadcasted_iota(jnp.int32, (count, lanes), 0).astype(jnp.float32)

    values = spline(row(3))[which]
    offset = rows(along_x.shape[0]) - (row(0) - (where_ref[0] * x_width).astype(jnp.float32))
    along_x[...] = place(offset, values)
    values = spline(row(4))[which]
    offset = lax.broadcasted_iota(jnp.int32, (mesh_size, lanes), 0) - row(1).astype(jnp.int32)
    high, low = split(place(offset & (mesh_size - 1), values))
    high_y[...] = high
    low_y[...] = low
    values = spline(row(5))[which]
    wave = rows(slots_padded) + (where_ref[1] * z_width).astype(jnp.float32)
    real = jnp.zeros_like(wave)
    imag = jnp.zeros_like(wave)
    cos, sin = turn(wave * row(2), mesh_size)
    by_cos, by_sin = turn(wave[:, 0:128], mesh_size)
    by_cos = jnp.concatenate([by_cos] * (lanes // 128), axis=1)
    by_sin = jnp.concatenate([by_sin] * (lanes // 128), axis=1)
    for k in range(4):
        if k:
            cos, sin = cos * by_cos - sin * by_sin, sin * by_cos + cos * by_sin
        real = real + (charge * values[k]) * cos
        imag = imag - (charge * values[k]) * sin
    along_z[0:slots_padded, :] = real
    along_z[slots_padded:, :] = imag


def groups(count, size):
    return [(low, min(low + size, count)) for low in range(0, count, size)]


def spread_kernel(first, count, slots_padded, wx, zq, bwh, bwl, rh, rl, ih, il, out, *sums):
    step = pl.program_id(0)
    padded = -(-count // 8) * 8
    width = sums[0].shape[0] - PAST * padded
    width = width // count
    wide = wx[0:width, :]
    right = (bwh[...], bwl[...])

    @pl.when(step == 0)
    def _():
        for acc in sums:
            acc[...] = jnp.zeros_like(acc)

    for low, high in groups(count, SPREAD_GROUP):
        pieces = []
        for c in range(2):
            base = c * slots_padded + first
            pieces += [wide * zq[base + g : base + g + 1, :] for g in range(low, high)]
            if high == count:
                strip = zq[base : base + padded, :]
                pieces += [wx[width + i : width + i + 1, :] * strip for i in range(PAST)]
        part = dot3(split(jnp.concatenate(pieces, axis=0)), right, 1)
        rows = part.shape[0] // 2
        for c in range(2):
            sums[c][low * width : low * width + rows, :] += part[c * rows : (c + 1) * rows]

    @pl.when(step == pl.num_programs(0) - 1)
    def _():
        real, imag = (split(acc[...]) for acc in sums)
        lines = dot3(real, (rh[...], rl[...])) + dot3(imag, (ih[...], il[...]))
        lanes = out.shape[2]
        for s in range(out.shape[0]):
            out[s] = lines[:, s * lanes : (s + 1) * lanes]


def influence_kernel(first, half, scale, where_ref, own, across, edge, flip, same, back, out):
    count, _, lanes = out.shape
    width = own.shape[1]
    lowest = half - max(first + count - 1, 1)
    both_flip = jnp.concatenate([flip[...]] * 2, axis=1)
    mirror = []
    for g in range(count):
        at = half - max(first + g, 1)
        pair = jnp.concatenate(split(across[at - lowest]), axis=0)
        turned = dot(both_flip, pair)
        lines = lax.broadcasted_iota(jnp.int32, turned.shape, 0) % width
        turned = jnp.where(lines == 0, edge[at], turned)
        mirror.append(turned if first + g > 0 else jnp.zeros_like(turned))
    plain = [own[first + g] for g in range(count) for _ in range(2)]
    plain = split(jnp.concatenate(plain, axis=0))
    mirror = split(jnp.concatenate(mirror, axis=0))
    left = jnp.concatenate([same[...]] * 2 + [back[...]] * 2, axis=1)
    values = dot(left, jnp.concatenate(plain + mirror, axis=1), 1)
    for g in range(count):
        keep = scale
        if first + g == half:
            keep = jnp.where(where_ref[2] == 1, scale, 0.0)
        out[g] = values[:, g * lanes : (g + 1) * lanes] * keep


def filter_kernel(lines, factor, th, tl, out):
    sects, extent, lanes = lines.shape
    count, mesh_size, _ = factor.shape
    width = mesh_size // sects
    past = count * width
    padded = (extent - past) // PAST
    empty = jnp.zeros((8 - PAST, lanes), jnp.float32)
    table = (th[...], tl[...])
    columns = []
    for g in range(count):
        pieces = []
        for s in range(sects):
            before = [past + i * padded + g for i in range(PAST)]
            before = [lines[(s - 1) % sects, at : at + 1, :] for at in before]
            at = g * width
            pieces.append(lines[s, at : at + 8, :] + jnp.concatenate(before + [empty], axis=0))
            pieces.append(lines[s, at + 8 : at + width, :])
        columns.append(jnp.concatenate(pieces, axis=0))
    both = dot3(table, split(jnp.concatenate(columns, axis=1)))
    half = lanes // 2
    sign = jnp.where(
        lax.broadcasted_iota(jnp.int32, (mesh_size, lanes), 1) < half, 1.0, -1.0
    )
    columns = []
    for g in range(count):
        cos = both[0:mesh_size, g * lanes : (g + 1) * lanes]
        sin = both[mesh_size:, g * lanes : (g + 1) * lanes]
        columns.append((cos + sign * pltpu.roll(sin, half, 1)) * factor[g])
    both = dot3(table, split(jnp.concatenate(columns, axis=1)))
    out[:, past:, :] = jnp.zeros((sects, extent - past, lanes), jnp.float32)
    for g in range(count):
        cos = both[0:mesh_size, g * lanes : (g + 1) * lanes]
        sin = both[mesh_size:, g * lanes : (g + 1) * lanes]
        field = cos - sign * pltpu.roll(sin, half, 1)
        for s in range(sects):
            after = ((s + 1) % sects) * width
            out[s, g * width : (g + 1) * width, :] = field[s * width : (s + 1) * width]
            for i in range(PAST):
                at = past + i * padded + g
                out[s, at : at + 1, :] = field[after + i : after + i + 1]


def gather_kernel(first, count, slots_padded, lines, bh, bl, wx, vx, zq, zv, bwh, bwl, bvh, bvl, *rest):
    *earlier, out, eh, el = rest
    sects, extent, lanes = lines.shape
    mesh_size = bwh.shape[0]
    width = mesh_size // sects
    past = count * width
    padded = (extent - past) // PAST

    @pl.when(pl.program_id(0) == 0)
    def _():
        joined = jnp.concatenate([lines[s] for s in range(sects)], axis=1)
        field = dot3(split(joined), (bh[...], bl[...]))
        pieces = []
        for g in range(count):
            for c in range(2):
                line = field[g * width : (g + 1) * width, c * mesh_size : (c + 1) * mesh_size]
                pieces.append(line)
        pieces += [field[past:, c * mesh_size : (c + 1) * mesh_size] for c in range(2)]
        high, low = split(jnp.concatenate(pieces, axis=0))
        eh[...] = high
        el[...] = low

    weights = (bwh[...], bwl[...])
    slopes = (bvh[...], bvl[...])
    steps = wx.shape[1]
    sums = [jnp.zeros((width, steps), jnp.float32) for _ in range(3)]
    strips = [[jnp.zeros((padded, steps), jnp.float32)] * PAST for _ in range(3)]
    for low, high in groups(count, GATHER_GROUP):
        part = slice(2 * low * width, 2 * (high * width if high < count else extent))
        left = (eh[part, :], el[part, :])
        along = dot3(left, weights)
        slope = dot3(left, slopes)
        for g in range(low, high):
            for c in range(2):
                at = c * slots_padded + first + g
                base = (2 * (g - low) + c) * width
                line = along[base : base + width]
                sums[0] = sums[0] + line * zq[at : at + 1, :]
                sums[1] = sums[1] + slope[base : base + width] * zq[at : at + 1, :]
                sums[2] = sums[2] + line * zv[at : at + 1, :]
        if high == count:
            for c in range(2):
                at = c * slots_padded + first
                for i in range(PAST):
                    base = 2 * (high - low) * width + (c * PAST + i) * padded
                    line = along[base : base + padded]
                    other = slope[base : base + padded]
                    strips[0][i] = strips[0][i] + line * zq[at : at + padded, :]
                    strips[1][i] = strips[1][i] + other * zq[at : at + padded, :]
                    strips[2][i] = strips[2][i] + line * zv[at : at + padded, :]
    forces = []
    for body, strip, shape in zip(sums, strips, (vx, wx, wx)):
        force = jnp.sum(body * shape[0:width, :], axis=0, keepdims=True)
        for i in range(PAST):
            at = width + i
            force = force + shape[at : at + 1, :] * jnp.sum(strip[i], axis=0, keepdims=True)
        forces.append(-force)
    result = jnp.concatenate(forces + [jnp.zeros_like(forces[0])], axis=0)
    width = out.shape[2]
    for d in range(out.shape[0]):
        part = result[:, d * width : (d + 1) * width]
        out[d] = part + earlier[0][d] if earlier else part


def cost(micros):
    return pl.CostEstimate(flops=int(micros * 1.0e9), transcendentals=0, bytes_accessed=int(micros * 1.0e5))


def params():
    return pltpu.CompilerParams(vmem_limit_bytes=VMEM)


def whole(array):
    return pl.BlockSpec(array.shape, lambda *_: (0,) * array.ndim)


def along_atoms(rows, step):
    return pl.BlockSpec((rows, step), lambda n: (0, n))


SMEM = pl.BlockSpec(memory_space=pltpu.SMEM)
IN_VMEM = pl.BlockSpec(memory_space=pltpu.VMEM)


def near_core(array):
    return pltpu.with_memory_space_constraint(array, pltpu.VMEM)


def pair_kernel(centre, others, mesh_size):
    half_mesh = float(mesh_size // 2)
    displace = []
    for component in range(3):
        offset = centre[component][None, :, None] - others[component][:, None, :]
        wrapped = jnp.mod(offset + half_mesh, float(mesh_size)) - half_mesh
        displace.append(
            wrapped + (centre[component + 3][None, :, None] - others[component + 3][:, None, :])
        )
    square = (
        displace[0] * displace[0]
        + displace[1] * displace[1]
        + displace[2] * displace[2]
        + soft_square
    )
    distance = jnp.sqrt(square)
    kernel = (
        lax.erfc(ewald_beta * distance) / (square * distance)
        + 2.0
        * ewald_beta
        / math.sqrt(math.pi)
        * jnp.exp(-ewald_beta * ewald_beta * square)
        / square
    )
    coupling = centre[6][None, :, None] * others[6][:, None, :] * kernel
    return jnp.stack([jnp.sum(coupling * shift_vector, axis=(0, 2)) for shift_vector in displace])


def shards(cells, fracs, charges, pair_blocks, influence):
    sects = lax.axis_size("sect")
    doms = lax.axis_size("dom")
    sect = lax.axis_index("sect")
    dom = lax.axis_index("dom")
    z_width, x_width, mesh_size = influence.shape
    atom_count = charges.shape[2]
    block_count = atom_count // BLOCK
    listed_count = pair_blocks.shape[3]
    half = z_width // 2
    slots = half + 1
    firsts = [-(-slots * n // CHUNKS) for n in range(CHUNKS + 1)]
    counts = [b - a for a, b in zip(firsts, firsts[1:])]
    padded = [-(-count // 8) * 8 for count in counts]
    slots_padded = -(-max(a + b for a, b in zip(firsts, padded)) // 8) * 8
    lanes = 2 * x_width
    total = doms * atom_count
    where_am_i = jnp.stack([sect, dom, (dom >= doms // 2).astype(jnp.int32)])

    f32, bf16 = jnp.float32, jnp.bfloat16
    copies = pl.pallas_call(
        pack_kernel,
        out_shape=jax.ShapeDtypeStruct((doms, block_count, 8, BLOCK), f32),
        name="pack",
    )(cells, fracs, charges)
    row = lax.all_to_all(copies, "dom", 0, 0, tiled=True)

    edges = []
    for s in range(sects):
        for d in range(doms):
            edges.append((s * doms + d, ((sects - s) % sects) * doms + doms - 1 - d))
    flip = np.zeros((2 * x_width, x_width), np.float32)
    for i in range(1, x_width):
        flip[i, x_width - i] = 1.0
        flip[x_width + i, x_width - i] = 1.0
    same = np.eye(mesh_size, dtype=np.float32)
    back = np.roll(same[::-1], 1, axis=0)
    flip, same, back = (jnp.asarray(m).astype(jnp.bfloat16) for m in (flip, same, back))
    planes = []
    for first, count in zip(firsts, counts):
        lowest = half - max(first + count - 1, 1)
        highest = half - max(first, 1)
        planes.append(influence[half + lowest : half + highest + 1])
    sect_flip = [(s, sects - 1 - s) for s in range(sects)]
    dom_flip = [(d, doms - 1 - d) for d in range(doms)]
    planes = [lax.ppermute(p, "sect", sect_flip) for p in planes]

    step = np.arange(mesh_size)
    angle = 2.0 * np.pi * (np.outer(step, step) % mesh_size) / mesh_size
    cos, sin = np.cos(angle), np.sin(angle)

    def by_sect(real, imag):
        real = real.reshape(mesh_size, sects, 1, x_width)
        imag = imag.reshape(mesh_size, sects, 1, x_width)
        return np.concatenate([real, imag], axis=2).reshape(mesh_size, 2 * mesh_size)

    rh, rl = split_table(by_sect(cos, -sin))
    ih, il = split_table(by_sect(sin, cos))
    bh, bl = split_table(np.concatenate([by_sect(cos, -sin).T, by_sect(sin, cos).T], axis=1))
    th, tl = split_table(np.concatenate([cos, sin], axis=0))

    atom_step = 2048
    grid = (total // atom_step,)
    shapes = [
        ((x_width + 8, total), f32),
        ((2 * slots_padded, total), f32),
        ((mesh_size, total), bf16),
        ((mesh_size, total), bf16),
    ]

    def basis(which, blocks):
        return pl.pallas_call(
            lambda *refs: basis_kernel(which, mesh_size, x_width, z_width, slots_padded, *refs),
            grid=grid,
            in_specs=[
                SMEM,
                pl.BlockSpec(
                    (atom_step // atom_count, block_count, 8, BLOCK), lambda n: (n, 0, 0, 0)
                ),
            ],
            out_specs=[along_atoms(shape[0], atom_step) for shape, _ in shapes],
            out_shape=[jax.ShapeDtypeStruct(shape, dtype) for shape, dtype in shapes],
            compiler_params=params(),
            cost_estimate=cost(0.1 if which else 4),
            name="basis",
        )(where_am_i, blocks)

    wx, zq, bwh, bwl = basis(0, row)

    sent = []
    for first, count in zip(firsts, counts):
        extent = count * x_width + PAST * (-(-count // 8) * 8)
        shape = (sects, extent, lanes)
        lines = pl.pallas_call(
            lambda *refs, first=first, count=count: spread_kernel(first, count, slots_padded, *refs),
            grid=grid,
            in_specs=[
                along_atoms(x_width + 8, atom_step),
                along_atoms(2 * slots_padded, atom_step),
                along_atoms(mesh_size, atom_step),
                along_atoms(mesh_size, atom_step),
            ]
            + [whole(t) for t in (rh, rl, ih, il)],
            out_specs=pl.BlockSpec(shape, lambda n: (0, 0, 0)),
            out_shape=jax.ShapeDtypeStruct(shape, f32),
            scratch_shapes=[pltpu.VMEM((extent, mesh_size), f32)] * 2,
            compiler_params=params(),
            cost_estimate=cost(9),
            name="spread",
        )(wx, zq, bwh, bwl, rh, rl, ih, il)
        sent.append(lines)
    later, beside, planes[0], sent[0] = lax.optimization_barrier(
        (influence, row, planes[0], sent[0])
    )
    corner = later[half:, 0:1]
    vx, zv, bvh, bvl = basis(1, beside)
    vx, sent[-1] = lax.optimization_barrier((vx, sent[-1]))
    planes[0] = lax.ppermute(planes[0], "dom", dom_flip)
    edge = lax.ppermute(corner, ("sect", "dom"), edges)
    sent = [lax.all_to_all(lines, "sect", split_axis=0, concat_axis=0, tiled=True) for lines in sent]
    planes[1:], beside, sent[0] = lax.optimization_barrier((planes[1:], beside, sent[0]))
    planes[1:] = [lax.ppermute(p, "dom", dom_flip) for p in planes[1:]]
    planes[0], edge, sent[0] = lax.optimization_barrier((planes[0], edge, sent[0]))
    ahead = [(s, (s + 1) % sects) for s in range(sects)]
    behind = [(b, a) for a, b in ahead]
    near = [lax.ppermute(beside, "sect", ahead), lax.ppermute(beside, "sect", behind)]

    def folded(first, count, mirror):
        return pl.pallas_call(
            lambda *refs: influence_kernel(first, half, float(mesh_size) ** -3, *refs),
            in_specs=[SMEM] + [pl.BlockSpec(memory_space=pltpu.VMEM)] * 6,
            out_specs=pl.BlockSpec(memory_space=pltpu.VMEM),
            out_shape=jax.ShapeDtypeStruct((count, mesh_size, lanes), f32),
            compiler_params=params(),
            cost_estimate=cost(3.5),
            name="influence",
        )(where_am_i, influence, mirror, near_core(edge), flip, same, back)

    factors = [folded(firsts[0], counts[0], planes[0])]
    for n in range(1, CHUNKS):
        factors.append(folded(firsts[n], counts[n], planes[n]))
    fields = []
    near, row, copies, sent[-1] = lax.optimization_barrier((near, row, copies, sent[-1]))
    packed = copies[0]
    for lines, factor in zip(sent, factors):
        field = pl.pallas_call(
            filter_kernel,
            grid=(1,),
            in_specs=[
                IN_VMEM,
                IN_VMEM,
                whole(th),
                whole(tl),
            ],
            out_specs=whole(lines),
            out_shape=jax.ShapeDtypeStruct(lines.shape, f32),
            compiler_params=params(),
            cost_estimate=cost(5.5),
            name="filter",
        )(near_core(lines), factor, th, tl)
        fields.append(field)
    fields = [lax.all_to_all(field, "sect", split_axis=0, concat_axis=0, tiled=True) for field in fields]

    listed = pair_blocks[0, 0]
    neighbour = listed // block_count
    near = jnp.stack([near[0], row, near[1]])
    from_dom = (dom + neighbour % 3 - 1) % doms
    source = (neighbour // 3 * doms + from_dom) * block_count + listed % block_count
    pool = near.reshape(3 * doms * block_count, 8 * BLOCK)
    pick = (source.reshape(-1, 1) == jnp.arange(pool.shape[0], dtype=jnp.int32)[None]).astype(f32)
    chosen = lax.dot_general(
        pick, pool, (((1,), (0,)), ((), ())), precision=lax.Precision.HIGHEST, preferred_element_type=f32
    ).reshape(block_count, listed_count, 8, BLOCK)
    chosen = jnp.transpose(chosen, (0, 2, 1, 3))
    block_forces = jnp.stack(
        [pair_kernel(packed[b], chosen[b], mesh_size) for b in range(block_count)], axis=1
    )
    short_force = block_forces.reshape(3, atom_count)

    earlier = []
    by_dom = pl.BlockSpec((atom_step // atom_count, 4, atom_count), lambda n: (n, 0, 0))
    for lines, first, count in zip(fields, firsts, counts):
        earlier = [pl.pallas_call(
            lambda *refs, first=first, count=count: gather_kernel(first, count, slots_padded, *refs),
            grid=grid,
            in_specs=[IN_VMEM, whole(bh), whole(bl)]
            + [along_atoms(a.shape[0], atom_step) for a in (wx, vx, zq, zv, bwh, bwl, bvh, bvl)]
            + [by_dom] * len(earlier),
            out_specs=by_dom,
            out_shape=jax.ShapeDtypeStruct((doms, 4, atom_count), f32),
            scratch_shapes=[pltpu.VMEM((2 * lines.shape[1], mesh_size), bf16)] * 2,
            compiler_params=params(),
            cost_estimate=cost(13),
            name="gather",
        )(near_core(lines), bh, bl, wx, vx, zq, zv, bwh, bwl, bvh, bvl, *earlier)]
    shares = lax.all_to_all(earlier[0], "dom", 0, 0, tiled=True)
    mesh_force = jnp.sum(shares, axis=0)[:3]
    return (short_force + mesh_force).reshape(3, 1, 1, atom_count)


def solution(mesh):
    in_specs = (
        P(None, "sect", "dom", None),
        P(None, "sect", "dom", None),
        P("sect", "dom", None),
        P("sect", "dom", None, None),
        P("dom", "sect", None),
    )
    out_specs = P(None, "sect", "dom", None)
    return jax.shard_map(shards, mesh=mesh, in_specs=in_specs, out_specs=out_specs, check_vma=False)
```
